256 devices in a mesh: dp: 16 (over z, core), expert: 16 (over y, x).
Axes of the slice: x: 4, y: 4, z: 8, core: 2. Of those that a mesh axis runs over, the one named last changes fastest.
Arguments:
- tokens: bfloat16 [32768, 1024], P(('dp', 'expert')), may hold values from -6 to 6
- out_grad: bfloat16 [32768, 1024], P(('dp', 'expert')), may hold values from -6 to 6
- route_ids: int32 [32768, 8], P(('dp', 'expert')), may hold values from 0 to 31, all different within a row; in each aligned block of 128 rows (0 to 127, 128 to 255, ...) at most 40 rows name the same one
- route_gates: float32 [32768, 8], P(('dp', 'expert')), may hold values from 0.2 to 1.8
- w_gate: bfloat16 [32, 1024, 512], P('expert', 'dp'), may hold values from -0.1875 to 0.1875
- w_up: bfloat16 [32, 1024, 512], P('expert', 'dp'), may hold values from -0.1875 to 0.1875
- w_down: bfloat16 [32, 512, 1024], P('expert', 'dp'), may hold values from -0.25 to 0.25
Outputs:
- input_grad: bfloat16 [32768, 1024], P(('dp', 'expert'))
- gate_grad: float32 [32768, 8], P(('dp', 'expert'))
- gate_wgrad: float32 [32, 1024, 512], P('expert', 'dp')
- up_wgrad: float32 [32, 1024, 512], P('expert', 'dp')
- down_wgrad: float32 [32, 512, 1024], P('expert', 'dp')
The draws below stay inside these ranges and needn't reach their ends.
Inputs may be any that keep to these rules, and one draw needn't show every extreme that they name: `route_ids`: each token names 8 different experts. Among the 128 tokens of one device at most 40 name any one expert, and in every draw some device has an expert named by exactly 40 of its tokens.
All inputs are finite; a program needn't handle non-finite values.
Results may differ from the reference program's by a relative error of at most 0.028.
Values may be sent and summed in bfloat16 or wider, within the bound.
No kernel may reach another device: no remote copies, remote signals or barrier semaphores. Data moves between devices by JAX's collectives and lax.ppermute only.
A program may use at most 128 MiB of HBM per device.

```python
import math
import jax
import jax.numpy as jnp
import numpy as np
from jax import lax

D = 1024
H = 512
TOPK = 8
EXP_DEV = 2
TOK_DEV = 128
EXPERTS = 32
CAP = 40
TOKENS = 32768
N_DP = 16
N_EXPERT = 16


def shard_levels(rng, dims, pieces, low, top_value):
    def one(axis_at, blocks):
        steps = jax.random.uniform(jax.random.fold_in(jax.random.fold_in(rng, 6), axis_at), (blocks,), jnp.float32, low / len(pieces), top_value / len(pieces))
        return jnp.repeat(jnp.exp(steps), dims[axis_at] // blocks).reshape((-1,) + (1,) * (len(dims) - axis_at - 1))

    factor_of = one(*pieces[0])
    for cut in pieces[1:]:
        factor_of = factor_of * one(*cut)
    return factor_of


def shared_out(own_key, own, number, rows, amount, top, bound, lean):
    ranking = jax.random.permutation(own_key, amount)
    crowded, common = shares(amount, rows * top, bound, lean, True), shares(amount, rows * top, bound, lean, False)
    places = jnp.arange(amount)

    def named(lengths, rotation):
        used = int((lengths > 0).sum())
        fixed = max(1, used // 4)
        shifted = fixed + (places - fixed + rotation * (used - fixed)) % max(1, amount - fixed)
        return jnp.zeros((amount,), jnp.int32).at[ranking[jnp.where(places < fixed, places, shifted)]].set(jnp.asarray(lengths, jnp.int32))

    lengths = jnp.where(number % 4 == 0, named(crowded, number // 4), named(common, number - number // 4 - 1))
    mixed = jax.random.permutation(jax.random.fold_in(own, 3), amount)
    source_of, receiver = mixed[0:amount // 2 * 2:2], mixed[1:amount // 2 * 2:2]
    margin = jnp.minimum(lengths[source_of] - 1, bound - lengths[receiver]) // 2
    margin = jnp.where((source_of == ranking[0]) | (receiver == ranking[0]) | (lengths[receiver] == 0), 0, jnp.maximum(margin, 0))
    shifted = jax.random.randint(jax.random.fold_in(own, 4), (amount // 2,), 0, 1 << 20) % (margin + 1)
    lengths = lengths.at[source_of].add(-shifted).at[receiver].add(shifted)
    members = jnp.searchsorted(jnp.cumsum(lengths), jnp.arange(rows * top), side="right").astype(jnp.int32)
    table = members.reshape(top, rows).T
    table = table[jax.random.permutation(jax.random.fold_in(own, 1), rows)]
    rotation = jax.random.randint(jax.random.fold_in(own, 2), (rows, 1), 0, top)
    return jnp.take_along_axis(table, (jnp.arange(top)[None, :] + rotation) % top, axis=1)


def shares(count, total, limit, skew, full):
    loads = [(1 << 20) // math.isqrt(grade ** skew) + 1 for grade in range(1, count + 1)]
    largest = limit if full else min(limit, max(-(-total // count), total * loads[0] // sum(loads)))
    least = 1 if total - largest >= count - 1 else 0
    given, rest = [largest] + [least] * (count - 1), total - largest - least * (count - 1)
    while rest > 0:
        candidates = [i for i in range(1, count) if given[i] < largest] or [i for i in range(1, count) if given[i] < limit]
        mass, left = sum([loads[i] for i in candidates]), rest
        for i in candidates:
            addition = min(limit - given[i], max(1, left * loads[i] // mass), rest)
            given[i] = given[i] + addition
            rest = rest - addition
    return np.array(given)


def scatter_about(rng, dims, scale, bound, split=(), kind=jnp.bfloat16):
    entries = jax.random.normal(rng, dims, jnp.float32) * scale
    if len(split) > 0:
        entries = shard_levels(rng, dims, split, -0.22, 0.18) * entries
    return jnp.clip(entries, min=-bound, max=bound).astype(kind)


def setup_inputs(seed: int = 0) -> dict:
    arg_keys = jax.random.split(jax.random.key(seed), 8)
    tokens = scatter_about(arg_keys[0], (TOKENS, D), 1.0, 6.0, ((0, 256),))
    out_grad = scatter_about(arg_keys[1], (TOKENS, D), 1.0, 6.0, ((0, 256),))
    route_ids_keys = jax.random.split(jax.random.fold_in(arg_keys[2], 1), TOKENS // TOK_DEV)
    route_ids_turns = jax.random.permutation(jax.random.fold_in(arg_keys[2], 3), TOKENS // TOK_DEV)
    route_ids = jax.vmap(lambda own, number: shared_out(jax.random.fold_in(arg_keys[2], 2), own, number, TOK_DEV, EXPERTS, TOPK, CAP, 2))(route_ids_keys, route_ids_turns).reshape((TOKENS, TOPK))
    route_gates = jnp.clip(0.2 + 1.5999999 * jax.random.uniform(arg_keys[3], (TOKENS, TOPK), jnp.float32) ** shard_levels(arg_keys[3], (TOKENS, TOPK), ((0, 256),), -0.2, 0.2), 0.2, 1.8)
    w_gate = scatter_about(arg_keys[4], (EXPERTS, D, H), D ** -0.5, 0.1875, ((0, 16), (1, 16)))
    w_up = scatter_about(arg_keys[5], (EXPERTS, D, H), D ** -0.5, 0.1875, ((0, 16), (1, 16)))
    w_down = scatter_about(arg_keys[6], (EXPERTS, H, D), H ** -0.5, 0.25, ((0, 16), (1, 16)))
    return {"tokens": tokens, "out_grad": out_grad, "route_ids": route_ids, "route_gates": route_gates, "w_gate": w_gate, "w_up": w_up, "w_down": w_down}


def slot_table(route_ids, experts, capacity):
    token_count, top_picks = route_ids.shape
    onehot = (route_ids[:, :, None] == jnp.arange(experts, dtype=jnp.int32)[None, None, :]).astype(jnp.int32)
    flat_hits = onehot.reshape(token_count * top_picks, experts)
    earlier = jnp.cumsum(flat_hits, axis=0) - flat_hits
    ranked = lax.optimization_barrier(jnp.sum(earlier * flat_hits, axis=1)).reshape(token_count, top_picks)
    return (route_ids * capacity + ranked).astype(jnp.int32)

def expert_rows(rows_in, grads_in, gates_in, w_gate, w_up, w_down):
    contract_rows = (((0,), (0,)), ((), ()))
    contract_last = (((1,), (1,)), ((), ()))
    gate_pre = jnp.dot(rows_in, w_gate, preferred_element_type=jnp.float32)
    up_proj = jnp.dot(rows_in, w_up, preferred_element_type=jnp.float32)
    sigmoid_gate = jax.nn.sigmoid(gate_pre)
    active = gate_pre * sigmoid_gate
    hidden = (active * up_proj).astype(jnp.bfloat16)
    output = jnp.dot(hidden, w_down, preferred_element_type=jnp.float32)
    copy_gate_grad = lax.optimization_barrier(jnp.sum(output * grads_in.astype(jnp.float32), axis=1))
    scaled = (gates_in[:, None] * grads_in.astype(jnp.float32)).astype(jnp.bfloat16)
    hidden_grad = lax.dot_general(scaled, w_down, contract_last, preferred_element_type=jnp.float32)
    up_grad = (hidden_grad * active).astype(jnp.bfloat16)
    pre_grad = (hidden_grad * up_proj * (sigmoid_gate * (1.0 + gate_pre * (1.0 - sigmoid_gate)))).astype(jnp.bfloat16)
    copy_input_grad = (lax.dot_general(pre_grad, w_gate, contract_last, preferred_element_type=jnp.float32) + lax.dot_general(up_grad, w_up, contract_last, preferred_element_type=jnp.float32)).astype(jnp.bfloat16)
    gate_part = lax.dot_general(rows_in, pre_grad, contract_rows, preferred_element_type=jnp.float32)
    up_part = lax.dot_general(rows_in, up_grad, contract_rows, preferred_element_type=jnp.float32)
    down_part = lax.dot_general(hidden, scaled, contract_rows, preferred_element_type=jnp.float32)
    return (copy_input_grad, copy_gate_grad, gate_part, up_part, down_part)

def reference(tokens, out_grad, route_ids, route_gates, w_gate, w_up, w_down):
    slot_rows = N_EXPERT * CAP
    copies = N_EXPERT * TOK_DEV * TOPK
    scale = 1.0 / math.sqrt(TOK_DEV * N_DP * TOPK / EXP_DEV)
    group_ids = route_ids.reshape(N_DP, N_EXPERT, TOK_DEV, TOPK)
    group_tokens = tokens.reshape(N_DP, N_EXPERT, TOK_DEV, D)
    group_grads = out_grad.reshape(N_DP, N_EXPERT, TOK_DEV, D)
    group_gates = route_gates.reshape(N_DP, N_EXPERT, TOK_DEV, TOPK)
    source = jnp.arange(N_EXPERT, dtype=jnp.int32)[:, None, None]

    def one_group(totals, inputs):
        ids_now, tokens_now, grads_now, gates_now = inputs
        slot_ids = jax.vmap(lambda block_ids: slot_table(block_ids, EXPERTS, CAP))(ids_now)
        ranked = slot_ids - ids_now * CAP
        position = (ids_now * slot_rows + source * CAP + ranked).reshape(copies).astype(jnp.int32)
        token_rows = jnp.broadcast_to(tokens_now[:, :, None, :], (N_EXPERT, TOK_DEV, TOPK, D)).reshape(copies, D)
        grad_rows = jnp.broadcast_to(grads_now[:, :, None, :], (N_EXPERT, TOK_DEV, TOPK, D)).reshape(copies, D)
        rows_in = jnp.zeros((EXPERTS * slot_rows, D), jnp.bfloat16).at[position].set(token_rows).reshape(EXPERTS, slot_rows, D)
        grads_in = jnp.zeros((EXPERTS * slot_rows, D), jnp.bfloat16).at[position].set(grad_rows).reshape(EXPERTS, slot_rows, D)
        gates_in = jnp.zeros((EXPERTS * slot_rows,), jnp.float32).at[position].set(gates_now.reshape(copies)).reshape(EXPERTS, slot_rows)
        parts = lax.map(lambda entry: expert_rows(entry[0], entry[1], entry[2], entry[3], entry[4], entry[5]), (rows_in, grads_in, gates_in, w_gate, w_up, w_down))
        input_copies = parts[0].reshape(EXPERTS * slot_rows, D)[position].reshape(N_EXPERT, TOK_DEV, TOPK, D)
        input_grad = lax.optimization_barrier(jnp.sum(input_copies.astype(jnp.float32), axis=2)).astype(jnp.bfloat16)
        gate_grad = parts[1].reshape(EXPERTS * slot_rows)[position].reshape(N_EXPERT, TOK_DEV, TOPK)
        rounded = lax.optimization_barrier((parts[2].astype(jnp.bfloat16), parts[3].astype(jnp.bfloat16), parts[4].astype(jnp.bfloat16)))
        gate_total = totals[0] + rounded[0].astype(jnp.float32)
        up_total = totals[1] + rounded[1].astype(jnp.float32)
        down_total = totals[2] + rounded[2].astype(jnp.float32)
        return ((gate_total, up_total, down_total), (input_grad, gate_grad))
    initial = (jnp.zeros((EXPERTS, D, H), jnp.float32), jnp.zeros((EXPERTS, D, H), jnp.float32), jnp.zeros((EXPERTS, H, D), jnp.float32))
    totals, outputs = lax.scan(one_group, initial, (group_ids, group_tokens, group_grads, group_gates))
    input_grad = outputs[0].reshape(TOKENS, D)
    gate_grad = outputs[1].reshape(TOKENS, TOPK)
    return (input_grad, gate_grad, totals[0] * scale, totals[1] * scale, totals[2] * scale)
```

```python
import math

import jax
import jax.numpy as jnp
from jax import lax
from jax.experimental import pallas as pl
from jax.experimental.pallas import tpu as pltpu
from jax.sharding import PartitionSpec as P

F32 = jnp.float32
BF16 = jnp.bfloat16
LANES = 128
VMEM_LIMIT = 56 * 1024 * 1024


def dot(a, b, ca, cb):
    return lax.dot_general(a, b, (((ca,), (cb,)), ((), ())), preferred_element_type=F32)


def split_high_low(x):
    high = x.astype(BF16)
    return high, (x - high.astype(F32)).astype(BF16)


def named_by_expert(ids, values, experts):
    top, tokens = ids.shape
    row = lax.broadcasted_iota(jnp.int32, (experts, tokens), 0)
    total = jnp.zeros((experts, tokens), F32)
    for k in range(top):
        total = total + jnp.where(ids[k : k + 1, :] == row, values[k : k + 1, :], 0.0)
    return total


def dispatch_kernel(ids_ref, gates_ref, tokens_ref, grads_ref, send_ref, slots_ref):
    experts, capacity, _ = send_ref.shape
    token_count, width = tokens_ref.shape
    ids = ids_ref[...]
    named = named_by_expert(ids, jnp.ones(ids.shape, F32), experts)
    gates = named_by_expert(ids, gates_ref[...], experts)
    earlier = lax.broadcasted_iota(jnp.int32, (token_count, token_count), 0)
    later = lax.broadcasted_iota(jnp.int32, (token_count, token_count), 1)
    before = jnp.where(earlier < later, 1.0, 0.0).astype(BF16)
    ranks = dot(named.astype(BF16), before, 1, 0)
    key = jnp.where(named > 0.0, ranks, -1.0)
    shape = (experts, capacity, token_count)
    place = lax.broadcasted_iota(jnp.int32, shape, 1).astype(F32)
    hit = key[:, None, :] == place
    slots = jnp.where(hit, 1.0, 0.0).reshape(experts * capacity, token_count).astype(BF16)
    slots_ref[...] = slots
    weighted = jnp.where(hit, gates[:, None, :], 0.0).reshape(experts * capacity, token_count)
    high, low = split_high_low(weighted)
    rows = dot(slots, tokens_ref[...], 1, 0)
    send_ref[:, :, :width] = rows.astype(BF16).reshape(experts, capacity, width)
    grads = grads_ref[...]
    both = jnp.concatenate([high, low], axis=1)
    scaled = dot(both, jnp.concatenate([grads, grads], axis=0), 1, 0)
    send_ref[:, :, width:] = scaled.astype(BF16).reshape(experts, capacity, width)


def expert_kernel(recv_ref, weights_ref, parts_ref, pre_ref, up_ref, gate_ref):
    sources, _, capacity, _ = recv_ref.shape
    pieces, _, depth, hidden_width = weights_ref.shape
    share = depth // 3
    half = share // 2
    rows_count = sources * capacity
    width = pieces * share

    def weight(start, size):
        return weights_ref[:, 0, start : start + size, :].reshape(pieces * size, hidden_width)

    w_gate = weight(0, share)
    w_up = weight(share, share)
    down_left = weight(2 * share, half)
    down_right = weight(2 * share + half, half)
    rows = recv_ref[:, 0, :, :width].reshape(rows_count, width)
    scaled = recv_ref[:, 0, :, width:].reshape(rows_count, width)
    cut = width // 2
    gate_pre = dot(rows, w_gate, 1, 0)
    up_proj = dot(rows, w_up, 1, 0)
    hidden_grad = dot(scaled[:, :cut], down_left, 1, 1) + dot(scaled[:, cut:], down_right, 1, 1)
    sig = jax.nn.sigmoid(gate_pre)
    act = gate_pre * sig
    hidden = (act * up_proj).astype(BF16)
    up_grad = (hidden_grad * act).astype(BF16)
    pre_grad = (hidden_grad * up_proj * (sig * (1.0 + gate_pre * (1.0 - sig)))).astype(BF16)
    pre_ref[0] = pre_grad
    up_ref[0] = up_grad
    gate_grad = jnp.sum(hidden.astype(F32) * hidden_grad, axis=1, keepdims=True)
    high, low = split_high_low(jnp.broadcast_to(gate_grad, (rows_count, LANES)))
    lane = lax.broadcasted_iota(jnp.int32, (rows_count, LANES), 1)
    gate_ref[0] = jnp.where(lane < LANES // 2, high.astype(F32), low.astype(F32)).astype(BF16)

    def put(start, size, value):
        parts_ref[:, 0, start : start + size, :] = value.astype(BF16).reshape(
            pieces, size, hidden_width
        )

    put(0, share, dot(rows, pre_grad, 0, 0))
    put(share, share, dot(rows, up_grad, 0, 0))
    put(2 * share, half, dot(hidden, scaled[:, :cut], 0, 0))
    put(2 * share + half, half, dot(hidden, scaled[:, cut:], 0, 0))


def input_kernel(pre_ref, up_ref, gate_ref, weights_ref, back_ref):
    sources, _, capacity, total_width = back_ref.shape
    pieces, _, depth, hidden_width = weights_ref.shape
    share = depth // 2
    width = pieces * share
    w_gate = weights_ref[:, 0, :share, :].reshape(width, hidden_width)
    w_up = weights_ref[:, 0, share:, :].reshape(width, hidden_width)
    grad = dot(pre_ref[0], w_gate, 1, 1) + dot(up_ref[0], w_up, 1, 1)
    back_ref[:, 0, :, :width] = grad.astype(BF16).reshape(sources, capacity, width)
    back_ref[:, 0, :, width:] = gate_ref[0].reshape(sources, capacity, total_width - width)


def combine_kernel(ids_ref, gates_ref, slots_ref, back_ref, input_ref, gate_ref):
    experts, capacity, _ = back_ref.shape
    top, token_count = ids_ref.shape
    width = input_ref.shape[1]
    slot_count = experts * capacity
    slots = slots_ref[...]
    rows = back_ref[:, :, :width].reshape(slot_count, width)
    input_ref[...] = dot(slots, rows, 0, 0).astype(BF16)
    extra = back_ref[:, :, width:].astype(F32)
    value = (extra[:, :, :1] + extra[:, :, LANES // 2 : LANES // 2 + 1]).reshape(slot_count, 1)
    picked = jnp.where(slots.astype(F32) > 0.0, value, 0.0)
    by_expert = jnp.sum(picked.reshape(experts, capacity, token_count), axis=1)
    row = lax.broadcasted_iota(jnp.int32, (experts, token_count), 0)
    ids = ids_ref[...]
    for k in range(top):
        own = jnp.where(ids[k : k + 1, :] == row, by_expert, 0.0)
        gate_ref[k : k + 1, :] = jnp.sum(own, axis=0, keepdims=True) / gates_ref[k : k + 1, :]


def shards(tokens, out_grad, route_ids, route_gates, w_gate, w_up, w_down):
    dp_size = lax.axis_size("dp")
    expert_size = lax.axis_size("expert")
    members, share, hidden_width = w_gate.shape
    half = share // 2
    experts = members * expert_size
    token_count, top = route_ids.shape
    width = tokens.shape[1]
    capacity = 5 * token_count * top // (4 * experts)
    slot_count = experts * capacity
    rows_count = expert_size * capacity
    scale = 1.0 / math.sqrt(token_count * dp_size * top / members)
    params = pltpu.CompilerParams(vmem_limit_bytes=VMEM_LIMIT)

    packed = jnp.concatenate(
        [w_gate, w_up, w_down[:, :, :hidden_width], w_down[:, :, hidden_width:]], axis=1
    )
    weights = lax.all_gather(packed, "dp", axis=0, tiled=False)

    ids = route_ids.T
    gates = route_gates.T
    send, slots = pl.pallas_call(
        dispatch_kernel,
        out_shape=(
            jax.ShapeDtypeStruct((experts, capacity, 2 * width), BF16),
            jax.ShapeDtypeStruct((slot_count, token_count), BF16),
        ),
        compiler_params=params,
        name="dispatch",
    )(ids, gates, tokens, out_grad)
    recv = lax.all_to_all(send, "expert", split_axis=0, concat_axis=0, tiled=True)
    recv = recv.reshape(expert_size, members, capacity, 2 * width)

    whole = lambda *shape: pl.BlockSpec(shape, lambda m: (0, m, 0, 0))
    own = lambda *shape: pl.BlockSpec(shape, lambda m: (m, 0, 0))
    depth = 3 * share
    parts, pre_grad, up_grad, gate_rows = pl.pallas_call(
        expert_kernel,
        grid=(members,),
        in_specs=[
            whole(expert_size, 1, capacity, 2 * width),
            whole(dp_size, 1, depth, hidden_width),
        ],
        out_specs=(
            whole(dp_size, 1, depth, hidden_width),
            own(1, rows_count, hidden_width),
            own(1, rows_count, hidden_width),
            own(1, rows_count, LANES),
        ),
        out_shape=(
            jax.ShapeDtypeStruct((dp_size, members, depth, hidden_width), BF16),
            jax.ShapeDtypeStruct((members, rows_count, hidden_width), BF16),
            jax.ShapeDtypeStruct((members, rows_count, hidden_width), BF16),
            jax.ShapeDtypeStruct((members, rows_count, LANES), BF16),
        ),
        compiler_params=params,
        name="expert",
    )(recv, weights)
    sums = lax.psum_scatter(parts, "dp", scatter_dimension=0, tiled=False)

    back = pl.pallas_call(
        input_kernel,
        grid=(members,),
        in_specs=[
            own(1, rows_count, hidden_width),
            own(1, rows_count, hidden_width),
            own(1, rows_count, LANES),
            whole(dp_size, 1, 2 * share, hidden_width),
        ],
        out_specs=whole(expert_size, 1, capacity, width + LANES),
        out_shape=jax.ShapeDtypeStruct((expert_size, members, capacity, width + LANES), BF16),
        compiler_params=params,
        name="inputs",
    )(pre_grad, up_grad, gate_rows, weights)
    back = lax.all_to_all(
        back.reshape(experts, capacity, width + LANES),
        "expert",
        split_axis=0,
        concat_axis=0,
        tiled=True,
    )
    input_grad, gate_grad = pl.pallas_call(
        combine_kernel,
        out_shape=(
            jax.ShapeDtypeStruct((token_count, width), BF16),
            jax.ShapeDtypeStruct((top, token_count), F32),
        ),
        compiler_params=params,
        name="combine",
    )(ids, gates, slots, back)

    sums = sums.astype(F32) * scale
    down = jnp.concatenate(
        [sums[:, 2 * share : 2 * share + half], sums[:, 2 * share + half :]], axis=2
    )
    return (input_grad, gate_grad.T, sums[:, :share], sums[:, share : 2 * share], down)


def solution(mesh):
    return jax.shard_map(
        shards,
        mesh=mesh,
        in_specs=(
            P(("dp", "expert"), None),
            P(("dp", "expert"), None),
            P(("dp", "expert"), None),
            P(("dp", "expert"), None),
            P("expert", "dp", None),
            P("expert", "dp", None),
            P("expert", "dp", None),
        ),
        out_specs=(
            P(("dp", "expert"), None),
            P(("dp", "expert"), None),
            P("expert", "dp", None),
            P("expert", "dp", None),
            P("expert", "dp", None),
        ),
        check_vma=False,
    )
```

```python
import functools
import math

import jax
import jax.numpy as jnp
from jax import lax
from jax.experimental import pallas as pl
from jax.experimental.pallas import tpu as pltpu
from jax.sharding import PartitionSpec as P

F32 = jnp.float32
BF16 = jnp.bfloat16
LANES = 128
VMEM_LIMIT = 56 * 1024 * 1024


def dot(a, b, ca, cb):
    return lax.dot_general(a, b, (((ca,), (cb,)), ((), ())), preferred_element_type=F32)


def split_high_low(x):
    high = x.astype(BF16)
    return high, (x - high.astype(F32)).astype(BF16)


def named_by_expert(ids, values, experts):
    top, tokens = ids.shape
    row = lax.broadcasted_iota(jnp.int32, (experts, tokens), 0)
    total = jnp.zeros((experts, tokens), F32)
    for k in range(top):
        total = total + jnp.where(ids[k : k + 1, :] == row, values[k : k + 1, :], 0.0)
    return total


def pack_weights(gate_ref, up_ref, down_ref, packed_ref):
    share = gate_ref.shape[1]
    half = share // 2
    hidden_width = gate_ref.shape[2]
    packed_ref[:, :share] = gate_ref[...]
    packed_ref[:, share : 2 * share] = up_ref[...]
    packed_ref[:, 2 * share : 2 * share + half] = down_ref[:, :, :hidden_width]
    packed_ref[:, 2 * share + half :] = down_ref[:, :, hidden_width:]


def dispatch_kernel(
    ids_ref,
    gates_ref,
    tokens_ref,
    grads_ref,
    w_gate_ref,
    w_up_ref,
    w_down_ref,
    send_ref,
    slots_ref,
    packed_ref,
):
    pack_weights(w_gate_ref, w_up_ref, w_down_ref, packed_ref)
    experts, capacity, _ = send_ref.shape
    token_count, width = tokens_ref.shape
    ids = ids_ref[...]
    named = named_by_expert(ids, jnp.ones(ids.shape, F32), experts)
    gates = named_by_expert(ids, gates_ref[...], experts)
    earlier = lax.broadcasted_iota(jnp.int32, (token_count, token_count), 0)
    later = lax.broadcasted_iota(jnp.int32, (token_count, token_count), 1)
    before = jnp.where(earlier < later, 1.0, 0.0).astype(BF16)
    ranks = dot(named.astype(BF16), before, 1, 0)
    key = jnp.where(named > 0.0, ranks, -1.0)
    shape = (experts, capacity, token_count)
    place = lax.broadcasted_iota(jnp.int32, shape, 1).astype(F32)
    hit = key[:, None, :] == place
    slots = jnp.where(hit, 1.0, 0.0).reshape(experts * capacity, token_count).astype(BF16)
    slots_ref[...] = slots
    weighted = jnp.where(hit, gates[:, None, :], 0.0).reshape(experts * capacity, token_count)
    high, low = split_high_low(weighted)
    rows = dot(slots, tokens_ref[...], 1, 0)
    send_ref[:, :, :width] = rows.astype(BF16).reshape(experts, capacity, width)
    grads = grads_ref[...]
    both = jnp.concatenate([high, low], axis=1)
    scaled = dot(both, jnp.concatenate([grads, grads], axis=0), 1, 0)
    send_ref[:, :, width:] = scaled.astype(BF16).reshape(experts, capacity, width)


def expert_kernel(
    core_ref, recv_ref, weights_ref, keep_ref, give_ref, pre_ref, up_ref, gate_ref
):
    sources, _, capacity, _ = recv_ref.shape
    pieces, _, depth, hidden_width = weights_ref.shape
    share = depth // 3
    half = share // 2
    rows_count = sources * capacity
    width = pieces * share

    def weight(start, size):
        return weights_ref[:, 0, start : start + size, :].reshape(pieces * size, hidden_width)

    w_gate = weight(0, share)
    w_up = weight(share, share)
    down_left = weight(2 * share, half)
    down_right = weight(2 * share + half, half)
    rows = recv_ref[:, 0, :, :width].reshape(rows_count, width)
    scaled = recv_ref[:, 0, :, width:].reshape(rows_count, width)
    cut = width // 2
    gate_pre = dot(rows, w_gate, 1, 0)
    up_proj = dot(rows, w_up, 1, 0)
    hidden_grad = dot(scaled[:, :cut], down_left, 1, 1) + dot(scaled[:, cut:], down_right, 1, 1)
    sig = jax.nn.sigmoid(gate_pre)
    act = gate_pre * sig
    hidden = (act * up_proj).astype(BF16)
    up_grad = (hidden_grad * act).astype(BF16)
    pre_grad = (hidden_grad * up_proj * (sig * (1.0 + gate_pre * (1.0 - sig)))).astype(BF16)
    pre_ref[0] = pre_grad
    up_ref[0] = up_grad
    gate_grad = jnp.sum(hidden.astype(F32) * hidden_grad, axis=1, keepdims=True)
    high, low = split_high_low(jnp.broadcast_to(gate_grad, (rows_count, LANES)))
    lane = lax.broadcasted_iota(jnp.int32, (rows_count, LANES), 1)
    gate_ref[0] = jnp.where(lane < LANES // 2, high.astype(F32), low.astype(F32)).astype(BF16)

    core = core_ref[0]

    def put(start, size, value):
        value = value.astype(BF16).reshape(pieces // 2, 2, size, hidden_width)

        @pl.when(core == 0)
        def _():
            keep_ref[:, 0, start : start + size, :] = value[:, 0]
            give_ref[:, 0, start : start + size, :] = value[:, 1]

        @pl.when(core == 1)
        def _():
            keep_ref[:, 0, start : start + size, :] = value[:, 1]
            give_ref[:, 0, start : start + size, :] = value[:, 0]

    put(0, share, dot(rows, pre_grad, 0, 0))
    put(share, share, dot(rows, up_grad, 0, 0))
    put(2 * share, half, dot(hidden, scaled[:, :cut], 0, 0))
    put(2 * share + half, half, dot(hidden, scaled[:, cut:], 0, 0))


def input_kernel(pre_ref, up_ref, gate_ref, weights_ref, back_ref):
    sources, _, capacity, total_width = back_ref.shape
    pieces, _, depth, hidden_width = weights_ref.shape
    share = depth // 2
    width = pieces * share
    w_gate = weights_ref[:, 0, :share, :].reshape(width, hidden_width)
    w_up = weights_ref[:, 0, share:, :].reshape(width, hidden_width)
    grad = dot(pre_ref[0], w_gate, 1, 1) + dot(up_ref[0], w_up, 1, 1)
    back_ref[:, 0, :, :width] = grad.astype(BF16).reshape(sources, capacity, width)
    back_ref[:, 0, :, width:] = gate_ref[0].reshape(sources, capacity, total_width - width)


def combine_kernel(ids_ref, gates_ref, slots_ref, back_ref, input_ref, gate_ref):
    experts, capacity, _ = back_ref.shape
    top, token_count = ids_ref.shape
    width = input_ref.shape[1]
    slot_count = experts * capacity
    slots = slots_ref[...]
    rows = back_ref[:, :, :width].reshape(slot_count, width)
    input_ref[...] = dot(slots, rows, 0, 0).astype(BF16)
    extra = back_ref[:, :, width:].astype(F32)
    value = (extra[:, :, :1] + extra[:, :, LANES // 2 : LANES // 2 + 1]).reshape(slot_count, 1)
    picked = jnp.where(slots.astype(F32) > 0.0, value, 0.0)
    by_expert = jnp.sum(picked.reshape(experts, capacity, token_count), axis=1)
    row = lax.broadcasted_iota(jnp.int32, (experts, token_count), 0)
    ids = ids_ref[...]
    for k in range(top):
        own = jnp.where(ids[k : k + 1, :] == row, by_expert, 0.0)
        gate_ref[k : k + 1, :] = jnp.sum(own, axis=0, keepdims=True) / gates_ref[k : k + 1, :]


def scale_kernel(scale, sums_ref, gate_ref, up_ref, down_ref):
    share = gate_ref.shape[1]
    half = share // 2
    hidden_width = gate_ref.shape[2]

    def part(start, size):
        return sums_ref[:, start : start + size].astype(F32) * scale

    gate_ref[...] = part(0, share)
    up_ref[...] = part(share, share)
    down_ref[:, :, :hidden_width] = part(2 * share, half)
    down_ref[:, :, hidden_width:] = part(2 * share + half, half)


def shards(tokens, out_grad, route_ids, route_gates, w_gate, w_up, w_down):
    dp_size = lax.axis_size("dp")
    expert_size = lax.axis_size("expert")
    members, share, hidden_width = w_gate.shape
    half = share // 2
    experts = members * expert_size
    token_count, top = route_ids.shape
    width = tokens.shape[1]
    capacity = 5 * token_count * top // (4 * experts)
    slot_count = experts * capacity
    rows_count = expert_size * capacity
    scale = 1.0 / math.sqrt(token_count * dp_size * top / members)
    params = pltpu.CompilerParams(vmem_limit_bytes=VMEM_LIMIT)

    ids = route_ids.T
    gates = route_gates.T
    depth = 3 * share
    send, slots, packed = pl.pallas_call(
        dispatch_kernel,
        out_shape=(
            jax.ShapeDtypeStruct((experts, capacity, 2 * width), BF16),
            jax.ShapeDtypeStruct((slot_count, token_count), BF16),
            jax.ShapeDtypeStruct((members, depth, hidden_width), BF16),
        ),
        compiler_params=params,
        name="dispatch",
    )(ids, gates, tokens, out_grad, w_gate, w_up, w_down)
    weights = lax.all_gather(packed, "dp", axis=0, tiled=False)
    recv = lax.all_to_all(send, "expert", split_axis=0, concat_axis=0, tiled=True)
    recv = recv.reshape(expert_size, members, capacity, 2 * width)

    whole = lambda *shape: pl.BlockSpec(shape, lambda m: (0, m, 0, 0))
    own = lambda *shape: pl.BlockSpec(shape, lambda m: (m, 0, 0))
    core = lax.rem(lax.axis_index("dp"), 2).astype(jnp.int32).reshape(1)
    keep, give, pre_grad, up_grad, gate_rows = pl.pallas_call(
        expert_kernel,
        grid=(members,),
        in_specs=[
            pl.BlockSpec(memory_space=pltpu.SMEM),
            whole(expert_size, 1, capacity, 2 * width),
            whole(dp_size, 1, depth, hidden_width),
        ],
        out_specs=(
            whole(dp_size // 2, 1, depth, hidden_width),
            whole(dp_size // 2, 1, depth, hidden_width),
            own(1, rows_count, hidden_width),
            own(1, rows_count, hidden_width),
            own(1, rows_count, LANES),
        ),
        out_shape=(
            jax.ShapeDtypeStruct((dp_size // 2, members, depth, hidden_width), BF16),
            jax.ShapeDtypeStruct((dp_size // 2, members, depth, hidden_width), BF16),
            jax.ShapeDtypeStruct((members, rows_count, hidden_width), BF16),
            jax.ShapeDtypeStruct((members, rows_count, hidden_width), BF16),
            jax.ShapeDtypeStruct((members, rows_count, LANES), BF16),
        ),
        compiler_params=params,
        name="expert",
    )(core, recv, weights)
    got = lax.ppermute(give, "dp", [(i, i ^ 1) for i in range(dp_size)])

    back = pl.pallas_call(
        input_kernel,
        grid=(members,),
        in_specs=[
            own(1, rows_count, hidden_width),
            own(1, rows_count, hidden_width),
            own(1, rows_count, LANES),
            whole(dp_size, 1, 2 * share, hidden_width),
        ],
        out_specs=whole(expert_size, 1, capacity, width + LANES),
        out_shape=jax.ShapeDtypeStruct((expert_size, members, capacity, width + LANES), BF16),
        compiler_params=params,
        name="inputs",
    )(pre_grad, up_grad, gate_rows, weights)
    pair_sum = keep + got
    same_core = [list(range(c, dp_size, 2)) for c in range(2)]
    sums = lax.psum_scatter(
        pair_sum, "dp", scatter_dimension=0, tiled=False, axis_index_groups=same_core
    )
    back = lax.all_to_all(
        back.reshape(experts, capacity, width + LANES),
        "expert",
        split_axis=0,
        concat_axis=0,
        tiled=True,
    )
    input_grad, gate_grad = pl.pallas_call(
        combine_kernel,
        out_shape=(
            jax.ShapeDtypeStruct((token_count, width), BF16),
            jax.ShapeDtypeStruct((top, token_count), F32),
        ),
        compiler_params=params,
        name="combine",
    )(ids, gates, slots, back)

    gate_sum, up_sum, down_sum = pl.pallas_call(
        functools.partial(scale_kernel, scale),
        out_shape=tuple(jax.ShapeDtypeStruct(w.shape, F32) for w in (w_gate, w_up, w_down)),
        compiler_params=params,
        name="scale",
    )(sums)
    return (input_grad, gate_grad.T, gate_sum, up_sum, down_sum)


def solution(mesh):
    return jax.shard_map(
        shards,
        mesh=mesh,
        in_specs=(
            P(("dp", "expert"), None),
            P(("dp", "expert"), None),
            P(("dp", "expert"), None),
            P(("dp", "expert"), None),
            P("expert", "dp", None),
            P("expert", "dp", None),
            P("expert", "dp", None),
        ),
        out_specs=(
            P(("dp", "expert"), None),
            P(("dp", "expert"), None),
            P("expert", "dp", None),
            P("expert", "dp", None),
            P("expert", "dp", None),
        ),
        check_vma=False,
    )
```

```python
import functools
import math

import jax
import jax.numpy as jnp
from jax import lax
from jax.experimental import pallas as pl
from jax.experimental.pallas import tpu as pltpu
from jax.sharding import PartitionSpec as P

F32 = jnp.float32
BF16 = jnp.bfloat16
LANES = 128
VMEM_LIMIT = 56 * 1024 * 1024
DISPATCH_STEPS = 4
EXPERT_STEPS = 4
INPUT_STEPS = 4


def dot(a, b, ca, cb):
    return lax.dot_general(a, b, (((ca,), (cb,)), ((), ())), preferred_element_type=F32)


def split_high_low(x):
    high = x.astype(BF16)
    return high, (x - high.astype(F32)).astype(BF16)


def expert_of_row(shape, members):
    row = lax.broadcasted_iota(jnp.int32, shape, 0)
    per_member = shape[0] // members
    return lax.rem(row, per_member) * members + row // per_member


def pack_weights(gate_ref, up_ref, down_ref, packed_ref):
    share = gate_ref.shape[1]
    half = share // 2
    hidden_width = gate_ref.shape[2]
    packed_ref[:, :share] = gate_ref[...]
    packed_ref[:, share : 2 * share] = up_ref[...]
    packed_ref[:, 2 * share : 2 * share + half] = down_ref[:, :, :hidden_width]
    packed_ref[:, 2 * share + half :] = down_ref[:, :, hidden_width:]


def dispatch_kernel(
    members,
    experts,
    ids_ref,
    gates_ref,
    tokens_ref,
    grads_ref,
    w_gate_ref,
    w_up_ref,
    w_down_ref,
    send_ref,
    slots_ref,
    packed_ref,
    key_ref,
    gate_ref,
):
    block, capacity, _ = send_ref.shape
    token_count, width = tokens_ref.shape
    step = pl.program_id(0)

    @pl.when(step == 0)
    def _():
        pack_weights(w_gate_ref, w_up_ref, w_down_ref, packed_ref)
        ids = ids_ref[...]
        expert = expert_of_row((experts, token_count), members)
        named = jnp.zeros((experts, token_count), F32)
        gates = jnp.zeros((experts, token_count), F32)
        for k in range(ids.shape[0]):
            same = ids[k : k + 1, :] == expert
            named = named + jnp.where(same, 1.0, 0.0)
            gates = gates + jnp.where(same, gates_ref[k : k + 1, :], 0.0)
        earlier = lax.broadcasted_iota(jnp.int32, (token_count, token_count), 0)
        later = lax.broadcasted_iota(jnp.int32, (token_count, token_count), 1)
        before = jnp.where(earlier < later, 1.0, 0.0).astype(BF16)
        ranks = dot(named.astype(BF16), before, 1, 0)
        key_ref[...] = jnp.where(named > 0.0, ranks, -1.0)
        gate_ref[...] = gates

    start = pl.multiple_of(step * block, block)
    key = key_ref[pl.ds(start, block), :]
    gates = gate_ref[pl.ds(start, block), :]
    place = lax.broadcasted_iota(jnp.int32, (block, capacity, token_count), 1).astype(F32)
    hit = key[:, None, :] == place
    slots = jnp.where(hit, 1.0, 0.0).reshape(block * capacity, token_count).astype(BF16)
    slots_ref[...] = slots
    weighted = jnp.where(hit, gates[:, None, :], 0.0).reshape(block * capacity, token_count)
    high, low = split_high_low(weighted)
    rows = dot(slots, tokens_ref[...], 1, 0)
    send_ref[:, :, :width] = rows.astype(BF16).reshape(block, capacity, width)
    grads = grads_ref[...]
    both = jnp.concatenate([high, low], axis=1)
    scaled = dot(both, jnp.concatenate([grads, grads], axis=0), 1, 0)
    send_ref[:, :, width:] = scaled.astype(BF16).reshape(block, capacity, width)


def expert_kernel(
    steps,
    core_ref,
    recv_ref,
    weights_ref,
    parts_ref,
    grads_ref,
    gate_ref,
    rows_all,
    scaled_all,
    grads_all,
    hidden_all,
):
    sources, capacity, _ = recv_ref.shape
    pieces, _, depth, hidden_width = weights_ref.shape
    share = depth // 3
    half = share // 2
    count = sources * capacity
    width = pieces * share
    step = pl.program_id(0)

    def weight(start, size):
        return weights_ref[:, 0, start : start + size, :].reshape(pieces * size, hidden_width)

    @pl.when(step < steps)
    def _():
        where = pl.ds(pl.multiple_of(step * count, count), count)
        rows = recv_ref[:, :, :width].reshape(count, width)
        scaled = recv_ref[:, :, width:].reshape(count, width)
        rows_all[where, :] = rows
        scaled_all[where, :] = scaled
        down = jnp.concatenate([weight(2 * share, half), weight(2 * share + half, half)], axis=1)
        gate_pre = dot(rows, weight(0, share), 1, 0)
        up_proj = dot(rows, weight(share, share), 1, 0)
        hidden_grad = dot(scaled, down, 1, 1)
        sig = jax.nn.sigmoid(gate_pre)
        act = gate_pre * sig
        hidden = (act * up_proj).astype(BF16)
        up_grad = (hidden_grad * act).astype(BF16)
        pre_grad = (hidden_grad * up_proj * (sig * (1.0 + gate_pre * (1.0 - sig)))).astype(BF16)
        grads = jnp.concatenate([pre_grad, up_grad], axis=1)
        grads_ref[...] = grads
        grads_all[where, :] = grads
        hidden_all[where, :] = hidden
        gate_grad = jnp.sum(hidden.astype(F32) * hidden_grad, axis=1, keepdims=True)
        high, low = split_high_low(jnp.broadcast_to(gate_grad, (count, LANES)))
        lane = lax.broadcasted_iota(jnp.int32, (count, LANES), 1)
        gate_ref[...] = jnp.where(lane < LANES // 2, high.astype(F32), low.astype(F32)).astype(BF16)

    for k in range(2):

        @pl.when(step == steps + k)
        def _(k=k):
            own = grads_all[:, k * hidden_width : (k + 1) * hidden_width]
            total = dot(rows_all[...], own, 0, 0).astype(BF16)
            parts_ref[...] = total.reshape(pieces, share, hidden_width)

    @pl.when(step == steps + 2)
    def _():
        total = dot(hidden_all[...], scaled_all[...], 0, 0).astype(BF16)
        parts_ref[:, :half, :] = total[:, :hidden_width].reshape(pieces, half, hidden_width)
        parts_ref[:, half:, :] = total[:, hidden_width:].reshape(pieces, half, hidden_width)


def input_kernel(core_ref, grads_ref, gate_ref, weights_ref, back_ref):
    sources, capacity, total_width = back_ref.shape
    pieces, _, depth, hidden_width = weights_ref.shape
    share = depth // 2
    width = pieces * share
    w_gate = weights_ref[:, 0, :share, :].reshape(width, hidden_width)
    w_up = weights_ref[:, 0, share:, :].reshape(width, hidden_width)
    grad = dot(grads_ref[...], jnp.concatenate([w_gate, w_up], axis=1), 1, 1)
    back_ref[:, :, :width] = grad.astype(BF16).reshape(sources, capacity, width)
    back_ref[:, :, width:] = gate_ref[...].reshape(sources, capacity, total_width - width)


def combine_kernel(members, ids_ref, gates_ref, slots_ref, back_ref, input_ref, gate_ref):
    experts, capacity, _ = back_ref.shape
    top, token_count = ids_ref.shape
    width = input_ref.shape[1]
    slot_count = experts * capacity
    slots = slots_ref[...]
    rows = back_ref[:, :, :width].reshape(slot_count, width)
    input_ref[...] = dot(slots, rows, 0, 0).astype(BF16)
    extra = back_ref[:, :, width:].astype(F32)
    value = (extra[:, :, :1] + extra[:, :, LANES // 2 : LANES // 2 + 1]).reshape(slot_count, 1)
    picked = jnp.where(slots.astype(F32) > 0.0, value, 0.0)
    by_expert = jnp.sum(picked.reshape(experts, capacity, token_count), axis=1)
    expert = expert_of_row((experts, token_count), members)
    ids = ids_ref[...]
    for k in range(top):
        own = jnp.where(ids[k : k + 1, :] == expert, by_expert, 0.0)
        gate_ref[k : k + 1, :] = jnp.sum(own, axis=0, keepdims=True) / gates_ref[k : k + 1, :]


def scale_kernel(scale, core_ref, sums_ref, got_ref, gate_ref, up_ref, down_ref):
    share = gate_ref.shape[1]
    half = share // 2
    hidden_width = gate_ref.shape[2]
    core = core_ref[0]

    def put(member, value):
        value = value.astype(F32) * scale
        gate_ref[member] = value[:share]
        up_ref[member] = value[share : 2 * share]
        down_ref[member, :, :hidden_width] = value[2 * share : 2 * share + half]
        down_ref[member, :, hidden_width:] = value[2 * share + half :]

    for c in range(2):

        @pl.when(core == c)
        def _(c=c):
            put(c, sums_ref[c])
            put(1 - c, got_ref[...])


def shards(tokens, out_grad, route_ids, route_gates, w_gate, w_up, w_down):
    dp_size = lax.axis_size("dp")
    expert_size = lax.axis_size("expert")
    members, share, hidden_width = w_gate.shape
    experts = members * expert_size
    chips = dp_size // members
    depth = 3 * share
    token_count, top = route_ids.shape
    width = tokens.shape[1]
    capacity = 5 * token_count * top // (4 * experts)
    slot_count = experts * capacity
    scale = 1.0 / math.sqrt(token_count * dp_size * top / members)
    params = pltpu.CompilerParams(vmem_limit_bytes=VMEM_LIMIT)

    core = lax.rem(lax.axis_index("dp"), members).astype(jnp.int32).reshape(1)
    first = core[0] == 0
    ids, core, first = lax.optimization_barrier((route_ids.T, core, first))
    gates = route_gates.T
    blocks = DISPATCH_STEPS
    block = experts // blocks
    full = lambda *shape: pl.BlockSpec(shape, lambda i: (0,) * len(shape))
    send, slots, packed = pl.pallas_call(
        functools.partial(dispatch_kernel, members, experts),
        grid=(blocks,),
        in_specs=[
            full(*x.shape) for x in (ids, gates, tokens, out_grad, w_gate, w_up, w_down)
        ],
        out_specs=(
            pl.BlockSpec((block, capacity, 2 * width), lambda i: (i, 0, 0)),
            pl.BlockSpec((block * capacity, token_count), lambda i: (i, 0)),
            full(members, depth, hidden_width),
        ),
        out_shape=(
            jax.ShapeDtypeStruct((experts, capacity, 2 * width), BF16),
            jax.ShapeDtypeStruct((slot_count, token_count), BF16),
            jax.ShapeDtypeStruct((members, depth, hidden_width), BF16),
        ),
        scratch_shapes=[pltpu.VMEM((experts, token_count), F32)] * 2,
        compiler_params=params,
        name="dispatch",
    )(ids, gates, tokens, out_grad, w_gate, w_up, w_down)
    weights = lax.all_gather(packed, "dp", axis=0, tiled=False)

    chip_plane = [
        [(chip * members + c) * expert_size + e for c in range(members) for e in range(expert_size)]
        for chip in range(chips)
    ]

    def exchange(x):
        return lax.all_to_all(
            x,
            ("dp", "expert"),
            split_axis=0,
            concat_axis=0,
            tiled=True,
            axis_index_groups=chip_plane,
        )

    recv = exchange(send)

    steps = EXPERT_STEPS
    sources = experts // steps
    rows_count = sources * capacity
    last = steps - 1
    parts, row_grads, gate_rows = pl.pallas_call(
        functools.partial(expert_kernel, steps),
        grid_spec=pltpu.PrefetchScalarGridSpec(
            num_scalar_prefetch=1,
            grid=(steps + 3,),
            in_specs=[
                pl.BlockSpec(
                    (sources, capacity, 2 * width), lambda i, c: (jnp.minimum(i, last), 0, 0)
                ),
                pl.BlockSpec((dp_size, 1, depth, hidden_width), lambda i, c: (0, c[0], 0, 0)),
            ],
            out_specs=(
                pl.BlockSpec(
                    (dp_size, share, hidden_width), lambda i, c: (0, jnp.maximum(i - steps, 0), 0)
                ),
                pl.BlockSpec(
                    (rows_count, 2 * hidden_width), lambda i, c: (jnp.minimum(i, last), 0)
                ),
                pl.BlockSpec((rows_count, LANES), lambda i, c: (jnp.minimum(i, last), 0)),
            ),
            scratch_shapes=[
                pltpu.VMEM((slot_count, width), BF16),
                pltpu.VMEM((slot_count, width), BF16),
                pltpu.VMEM((slot_count, 2 * hidden_width), BF16),
                pltpu.VMEM((slot_count, hidden_width), BF16),
            ],
        ),
        out_shape=(
            jax.ShapeDtypeStruct((dp_size, depth, hidden_width), BF16),
            jax.ShapeDtypeStruct((slot_count, 2 * hidden_width), BF16),
            jax.ShapeDtypeStruct((slot_count, LANES), BF16),
        ),
        compiler_params=params,
        name="expert",
    )(core, recv, weights)
    same_core = [list(range(c, dp_size, members)) for c in range(members)]
    sums = lax.psum_scatter(
        parts.reshape(chips, members, depth, hidden_width),
        "dp",
        scatter_dimension=0,
        tiled=False,
        axis_index_groups=same_core,
    )

    steps = INPUT_STEPS
    sources = experts // steps
    rows_count = sources * capacity
    back = pl.pallas_call(
        input_kernel,
        grid_spec=pltpu.PrefetchScalarGridSpec(
            num_scalar_prefetch=1,
            grid=(steps,),
            in_specs=[
                pl.BlockSpec((rows_count, 2 * hidden_width), lambda i, c: (i, 0)),
                pl.BlockSpec((rows_count, LANES), lambda i, c: (i, 0)),
                pl.BlockSpec((dp_size, 1, 2 * share, hidden_width), lambda i, c: (0, c[0], 0, 0)),
            ],
            out_specs=pl.BlockSpec((sources, capacity, width + LANES), lambda i, c: (i, 0, 0)),
        ),
        out_shape=jax.ShapeDtypeStruct((experts, capacity, width + LANES), BF16),
        compiler_params=params,
        name="inputs",
    )(core, row_grads, gate_rows, weights)
    back, sums = lax.optimization_barrier((exchange(back), sums))
    other = jnp.where(first, sums[1], sums[0])
    got = lax.ppermute(other, "dp", [(i, i ^ 1) for i in range(dp_size)])
    input_grad, gate_grad = pl.pallas_call(
        functools.partial(combine_kernel, members),
        out_shape=(
            jax.ShapeDtypeStruct((token_count, width), BF16),
            jax.ShapeDtypeStruct((top, token_count), F32),
        ),
        compiler_params=params,
        name="combine",
    )(ids, gates, slots, back)

    gate_sum, up_sum, down_sum = pl.pallas_call(
        functools.partial(scale_kernel, scale),
        in_specs=[
            pl.BlockSpec(memory_space=pltpu.SMEM),
            pl.BlockSpec(memory_space=pltpu.VMEM),
            pl.BlockSpec(memory_space=pltpu.VMEM),
        ],
        out_shape=tuple(jax.ShapeDtypeStruct(w.shape, F32) for w in (w_gate, w_up, w_down)),
        compiler_params=params,
        name="scale",
    )(core, sums, got)
    return (input_grad, gate_grad.T, gate_sum, up_sum, down_sum)


def solution(mesh):
    return jax.shard_map(
        shards,
        mesh=mesh,
        in_specs=(
            P(("dp", "expert"), None),
            P(("dp", "expert"), None),
            P(("dp", "expert"), None),
            P(("dp", "expert"), None),
            P("expert", "dp", None),
            P("expert", "dp", None),
            P("expert", "dp", None),
        ),
        out_specs=(
            P(("dp", "expert"), None),
            P(("dp", "expert"), None),
            P("expert", "dp", None),
            P("expert", "dp", None),
            P("expert", "dp", None),
        ),
        check_vma=False,
    )
```

```python
import functools
import math

import jax
import jax.numpy as jnp
from jax import lax
from jax.experimental import pallas as pl
from jax.experimental.pallas import tpu as pltpu
from jax.sharding import PartitionSpec as P

F32 = jnp.float32
BF16 = jnp.bfloat16
MIB = 1024 * 1024
TILE = 8
PANEL = 256
CHUNKS = 4


def in_vmem(x):
    return pltpu.with_memory_space_constraint(x, pltpu.VMEM)


def in_hbm(x):
    return pltpu.with_memory_space_constraint(x, pltpu.HBM)


def vmem_result(*shape):
    return pltpu.VMEM(shape, BF16)


def hbm_result(*shape):
    return pltpu.HBM(shape, BF16)


def dot(a, b, ca, cb):
    return lax.dot_general(a, b, (((ca,), (cb,)), ((), ())), preferred_element_type=F32)


def split_high_low(x):
    high = x.astype(BF16)
    return high, (x - high.astype(F32)).astype(BF16)


def expert_of_row(shape, members):
    row = lax.broadcasted_iota(jnp.int32, shape, 0)
    per_member = shape[0] // members
    return lax.rem(row, per_member) * members + row // per_member


def weight_copies(gate_ref, up_ref, down_ref, packed_ref, sems):
    share = gate_ref.shape[1]
    half = share // 2
    hidden_width = gate_ref.shape[2]
    pieces = (
        (gate_ref, 0, share),
        (up_ref, share, share),
        (down_ref.at[:, :, :hidden_width], 2 * share, half),
        (down_ref.at[:, :, hidden_width:], 2 * share + half, half),
    )
    return [
        pltpu.make_async_copy(ref, packed_ref.at[:, start : start + size, :], sems.at[k])
        for k, (ref, start, size) in enumerate(pieces)
    ]


def dispatch_kernel(
    members,
    ids_ref,
    gates_ref,
    tokens_ref,
    grads_ref,
    w_gate_ref,
    w_up_ref,
    w_down_ref,
    send_ref,
    slots_ref,
    packed_ref,
    tokens_buf,
    grads_buf,
    send_buf,
    weight_sems,
    token_sems,
    send_sems,
):
    loads = [
        pltpu.make_async_copy(tokens_ref, tokens_buf, token_sems.at[0]),
        pltpu.make_async_copy(grads_ref, grads_buf, token_sems.at[1]),
    ]
    for copy in loads:
        copy.start()
    packing = weight_copies(w_gate_ref, w_up_ref, w_down_ref, packed_ref, weight_sems)
    for copy in packing:
        copy.start()
    experts, capacity, _ = send_buf.shape
    token_count, width = tokens_buf.shape
    ids = ids_ref[...]
    expert = expert_of_row((experts, token_count), members)
    named = jnp.zeros((experts, token_count), F32)
    gates = jnp.zeros((experts, token_count), F32)
    for k in range(ids.shape[0]):
        same = ids[k : k + 1, :] == expert
        named = named + jnp.where(same, 1.0, 0.0)
        gates = gates + jnp.where(same, gates_ref[k : k + 1, :], 0.0)
    earlier = lax.broadcasted_iota(jnp.int32, (token_count, token_count), 0)
    later = lax.broadcasted_iota(jnp.int32, (token_count, token_count), 1)
    before = jnp.where(earlier < later, 1.0, 0.0).astype(BF16)
    ranks = dot(named.astype(BF16), before, 1, 0)
    keys = jnp.where(named > 0.0, ranks, -1.0)
    for copy in loads:
        copy.wait()
    tokens = tokens_buf[...]
    grads = jnp.concatenate([grads_buf[...], grads_buf[...]], axis=0)
    block = experts // CHUNKS
    count = block * capacity
    place = lax.broadcasted_iota(jnp.int32, (block, capacity, token_count), 1).astype(F32)
    sends = []
    for i in range(CHUNKS):
        start = i * block
        hit = keys[start : start + block, None, :] == place
        slots = jnp.where(hit, 1.0, 0.0).reshape(count, token_count).astype(BF16)
        slots_ref[i * count : (i + 1) * count, :] = slots
        weighted = jnp.where(hit, gates[start : start + block, None, :], 0.0)
        high, low = split_high_low(weighted.reshape(count, token_count))
        rows = dot(slots, tokens, 1, 0)
        scaled = dot(jnp.concatenate([high, low], axis=1), grads, 1, 0)
        shape = (block, capacity, width)
        here = slice(start, start + block)
        send_buf[here, :, :width] = rows.astype(BF16).reshape(shape)
        send_buf[here, :, width:] = scaled.astype(BF16).reshape(shape)
        sends.append(
            pltpu.make_async_copy(send_buf.at[here], send_ref.at[here], send_sems.at[i])
        )
        sends[i].start()
    for copy in packing + sends:
        copy.wait()


def expert_kernel(
    core_ref,
    recv_ref,
    weights_ref,
    parts_ref,
    grads_ref,
    gate_ref,
    ins_ref,
    rows_ref,
    down_ref,
    hidden_ref,
    stage_ref,
    row_sems,
    in_sems,
    out_sems,
):
    sources, capacity, _ = rows_ref.shape
    pieces, _, depth, hidden_width = weights_ref.shape
    share = depth // 3
    half = share // 2
    slot_count = sources * capacity
    width = pieces * share
    core = core_ref[0]

    def fetch(k, target):
        return pltpu.make_async_copy(
            weights_ref.at[:, core, k * share : (k + 1) * share, :], target, in_sems.at[k]
        )

    fetches = [
        fetch(0, ins_ref.at[:, :, :hidden_width]),
        fetch(1, ins_ref.at[:, :, hidden_width:]),
        fetch(2, down_ref),
    ]
    block = sources // CHUNKS
    arrivals = [
        pltpu.make_async_copy(
            recv_ref.at[i * block : (i + 1) * block],
            rows_ref.at[i * block : (i + 1) * block],
            row_sems.at[i],
        )
        for i in range(CHUNKS)
    ]
    fetches[0].start()
    arrivals[0].start()
    fetches[1].start()
    fetches[2].start()
    fetches[0].wait()
    arrivals[0].wait()
    for copy in arrivals[1:]:
        copy.start()
    fetches[1].wait()
    fetches[2].wait()
    w_gate = ins_ref[:, :, :hidden_width].reshape(width, hidden_width)
    w_up = ins_ref[:, :, hidden_width:].reshape(width, hidden_width)
    down = jnp.concatenate(
        [
            down_ref[:, :half, :].reshape(hidden_width, hidden_width),
            down_ref[:, half:, :].reshape(hidden_width, hidden_width),
        ],
        axis=1,
    )
    count = block * capacity
    tiles = capacity // TILE
    lane = lax.broadcasted_iota(jnp.int32, (block, TILE, PANEL), 2)
    for i in range(CHUNKS):
        here = slice(i * block, (i + 1) * block)
        where = slice(i * count, (i + 1) * count)
        if i > 0:
            arrivals[i].wait()
        rows = rows_ref[here, :, :width].reshape(count, width)
        scaled = rows_ref[here, :, width:].reshape(count, width)
        gate_pre = dot(rows, w_gate, 1, 0)
        up_proj = dot(rows, w_up, 1, 0)
        hidden_grad = dot(scaled, down, 1, 1)
        sig = jax.nn.sigmoid(gate_pre)
        act = gate_pre * sig
        hidden = (act * up_proj).astype(BF16)
        hidden_ref[where, :] = hidden
        grads_ref[where, hidden_width:] = (hidden_grad * act).astype(BF16)
        pre_grad = hidden_grad * up_proj * (sig * (1.0 + gate_pre * (1.0 - sig)))
        grads_ref[where, :hidden_width] = pre_grad.astype(BF16)
        gate_grad = jnp.sum(hidden.astype(F32) * hidden_grad, axis=1, keepdims=True)
        gate_grad = gate_grad.reshape(block, tiles, TILE, 1)
        tile = jnp.zeros((block, TILE, PANEL), F32)
        for n in range(tiles):
            value = jnp.broadcast_to(gate_grad[:, n], (block, TILE, PANEL))
            high, low = split_high_low(value)
            tile = jnp.where(lane == 2 * n, high.astype(F32), tile)
            tile = jnp.where(lane == 2 * n + 1, low.astype(F32), tile)
        gate_ref[here] = tile.astype(BF16)

    def store(k):
        return pltpu.make_async_copy(
            stage_ref.at[k], parts_ref.at[:, k * share : (k + 1) * share, :], out_sems.at[k]
        )

    stores = [store(k) for k in range(3)]
    rows = rows_ref[:, :, :width].reshape(slot_count, width)
    for k in range(2):
        own = grads_ref[:, k * hidden_width : (k + 1) * hidden_width]
        total = dot(rows, own, 0, 0).astype(BF16)
        stage_ref[k] = total.reshape(pieces, share, hidden_width)
        stores[k].start()
    scaled = rows_ref[:, :, width:].reshape(slot_count, width)
    total = dot(hidden_ref[...], scaled, 0, 0).astype(BF16)
    stage_ref[2, :, :half, :] = total[:, :hidden_width].reshape(pieces, half, hidden_width)
    stage_ref[2, :, half:, :] = total[:, hidden_width:].reshape(pieces, half, hidden_width)
    stores[2].start()
    for copy in stores:
        copy.wait()


def input_kernel(core_ref, grads_ref, gate_ref, weights_ref, back_ref, ins_ref, sems):
    sources, panels, _, _ = back_ref.shape
    share = weights_ref.shape[2] // 3
    pieces, hidden_width = ins_ref.shape[0], ins_ref.shape[2] // 2
    core = core_ref[0]
    span = PANEL // share
    loads = []
    for n in range(pieces // span):
        here = slice(n * span, (n + 1) * span)
        for k in range(2):
            loads.append(
                pltpu.make_async_copy(
                    weights_ref.at[here, core, k * share : (k + 1) * share, :],
                    ins_ref.at[here, :, k * hidden_width : (k + 1) * hidden_width],
                    sems.at[n, k],
                )
            )
    for copy in loads:
        copy.start()
    back_ref[:, panels - 1] = gate_ref[...]
    grads = grads_ref[...]
    tiles = (panels - 1) * span // pieces
    for n in range(pieces // span):
        loads[2 * n].wait()
        loads[2 * n + 1].wait()
        weights = ins_ref[n * span : (n + 1) * span].reshape(PANEL, 2 * hidden_width)
        panel = dot(grads, weights, 1, 1).astype(BF16)
        back_ref[:, n * tiles : (n + 1) * tiles] = panel.reshape(sources, tiles, TILE, PANEL)


def combine_kernel(members, ids_ref, gates_ref, slots_ref, back_ref, input_ref, gate_ref):
    experts, panels, _, _ = back_ref.shape
    top, token_count = ids_ref.shape
    width = input_ref.shape[1]
    slot_count = slots_ref.shape[0]
    tiles = slot_count // (experts * TILE)
    slots = slots_ref[...]
    for n in range(width // PANEL):
        rows = back_ref[:, n * tiles : (n + 1) * tiles].reshape(slot_count, PANEL)
        input_ref[:, n * PANEL : (n + 1) * PANEL] = dot(slots, rows, 0, 0).astype(BF16)
    extra = back_ref[:, panels - 1].astype(F32)
    hits = slots.astype(F32).reshape(experts, tiles * TILE, token_count)
    by_expert = jnp.zeros((experts, token_count), F32)
    for n in range(tiles):
        value = extra[:, :, 2 * n : 2 * n + 1] + extra[:, :, 2 * n + 1 : 2 * n + 2]
        picked = jnp.where(hits[:, n * TILE : (n + 1) * TILE, :] > 0.0, value, 0.0)
        by_expert = by_expert + jnp.sum(picked, axis=1)
    expert = expert_of_row((experts, token_count), members)
    ids = ids_ref[...]
    for k in range(top):
        own = jnp.where(ids[k : k + 1, :] == expert, by_expert, 0.0)
        gate_ref[k : k + 1, :] = jnp.sum(own, axis=0, keepdims=True) / gates_ref[k : k + 1, :]


def scale_kernel(scale, core_ref, sums_ref, got_ref, gate_ref, up_ref, down_ref):
    share = gate_ref.shape[1]
    half = share // 2
    hidden_width = gate_ref.shape[2]
    core = core_ref[0]

    def put(member, value):
        value = value.astype(F32) * scale
        gate_ref[member] = value[:share]
        up_ref[member] = value[share : 2 * share]
        down_ref[member, :, :hidden_width] = value[2 * share : 2 * share + half]
        down_ref[member, :, hidden_width:] = value[2 * share + half :]

    for c in range(2):

        @pl.when(core == c)
        def _(c=c):
            put(c, sums_ref[c])
            put(1 - c, got_ref[...])


def shards(tokens, out_grad, route_ids, route_gates, w_gate, w_up, w_down):
    dp_size = lax.axis_size("dp")
    expert_size = lax.axis_size("expert")
    members, share, hidden_width = w_gate.shape
    experts = members * expert_size
    chips = dp_size // members
    depth = 3 * share
    token_count, top = route_ids.shape
    width = tokens.shape[1]
    capacity = 5 * token_count * top // (4 * experts)
    slot_count = experts * capacity
    scale = 1.0 / math.sqrt(token_count * dp_size * top / members)
    params = lambda mib: pltpu.CompilerParams(vmem_limit_bytes=mib * MIB)
    vmem = pl.BlockSpec(memory_space=pltpu.VMEM)
    smem = pl.BlockSpec(memory_space=pltpu.SMEM)
    anywhere = pl.BlockSpec(memory_space=pl.ANY)

    core = lax.rem(lax.axis_index("dp"), members).astype(jnp.int32).reshape(1)
    first = core[0] == 0
    ids, core, first = lax.optimization_barrier((route_ids.T, core, first))
    gates = route_gates.T
    send, slots, packed = pl.pallas_call(
        functools.partial(dispatch_kernel, members),
        in_specs=[vmem, vmem] + [anywhere] * 5,
        out_specs=(anywhere, vmem, anywhere),
        out_shape=(
            hbm_result(experts, capacity, 2 * width),
            vmem_result(slot_count, token_count),
            hbm_result(members, depth, hidden_width),
        ),
        scratch_shapes=[
            pltpu.VMEM((token_count, width), BF16),
            pltpu.VMEM((token_count, width), BF16),
            pltpu.VMEM((experts, capacity, 2 * width), BF16),
            pltpu.SemaphoreType.DMA((4,)),
            pltpu.SemaphoreType.DMA((2,)),
            pltpu.SemaphoreType.DMA((CHUNKS,)),
        ],
        compiler_params=params(24),
        name="dispatch",
    )(in_hbm(ids), in_hbm(gates), *map(in_hbm, (tokens, out_grad, w_gate, w_up, w_down)))
    weights = lax.all_gather(packed, "dp", axis=0, tiled=False)

    chip_plane = [
        [(chip * members + c) * expert_size + e for c in range(members) for e in range(expert_size)]
        for chip in range(chips)
    ]

    def exchange(x):
        return lax.all_to_all(
            x,
            ("dp", "expert"),
            split_axis=0,
            concat_axis=0,
            tiled=True,
            axis_index_groups=chip_plane,
        )

    recv = exchange(send)

    parts, row_grads, gate_tiles = pl.pallas_call(
        expert_kernel,
        in_specs=[smem, anywhere, anywhere],
        out_specs=(anywhere, vmem, vmem),
        out_shape=(
            hbm_result(dp_size, depth, hidden_width),
            vmem_result(slot_count, 2 * hidden_width),
            vmem_result(experts, TILE, PANEL),
        ),
        scratch_shapes=[
            pltpu.VMEM((dp_size, share, 2 * hidden_width), BF16),
            pltpu.VMEM((experts, capacity, 2 * width), BF16),
            pltpu.VMEM((dp_size, share, hidden_width), BF16),
            pltpu.VMEM((slot_count, hidden_width), BF16),
            pltpu.VMEM((3, dp_size, share, hidden_width), BF16),
            pltpu.SemaphoreType.DMA((CHUNKS,)),
            pltpu.SemaphoreType.DMA((3,)),
            pltpu.SemaphoreType.DMA((3,)),
        ],
        compiler_params=params(40),
        name="expert",
    )(core, in_hbm(recv), in_hbm(weights))
    same_core = [list(range(c, dp_size, members)) for c in range(members)]
    sums = lax.psum_scatter(
        parts.reshape(chips, members, depth, hidden_width),
        "dp",
        scatter_dimension=0,
        tiled=False,
        axis_index_groups=same_core,
    )

    panels = capacity * width // (TILE * PANEL) + 1
    back = pl.pallas_call(
        input_kernel,
        in_specs=[smem, vmem, vmem, anywhere],
        out_specs=vmem,
        out_shape=vmem_result(experts, panels, TILE, PANEL),
        scratch_shapes=[
            pltpu.VMEM((dp_size, share, 2 * hidden_width), BF16),
            pltpu.SemaphoreType.DMA((width // PANEL, 2)),
        ],
        compiler_params=params(24),
        name="inputs",
    )(core, in_vmem(row_grads), in_vmem(gate_tiles), in_hbm(weights))
    back, sums = lax.optimization_barrier((exchange(back), sums))
    other = jnp.where(first, sums[1], sums[0])
    got = lax.ppermute(other, "dp", [(i, i ^ 1) for i in range(dp_size)])
    input_grad, gate_grad = pl.pallas_call(
        functools.partial(combine_kernel, members),
        out_shape=(
            jax.ShapeDtypeStruct((token_count, width), BF16),
            jax.ShapeDtypeStruct((top, token_count), F32),
        ),
        compiler_params=params(24),
        name="combine",
    )(ids, gates, in_vmem(slots), in_vmem(back))

    gate_sum, up_sum, down_sum = pl.pallas_call(
        functools.partial(scale_kernel, scale),
        in_specs=[smem, vmem, vmem],
        out_shape=tuple(jax.ShapeDtypeStruct(w.shape, F32) for w in (w_gate, w_up, w_down)),
        compiler_params=params(16),
        name="scale",
    )(core, sums, in_vmem(got))
    return (input_grad, gate_grad.T, gate_sum, up_sum, down_sum)


def solution(mesh):
    return jax.shard_map(
        shards,
        mesh=mesh,
        in_specs=(
            P(("dp", "expert"), None),
            P(("dp", "expert"), None),
            P(("dp", "expert"), None),
            P(("dp", "expert"), None),
            P("expert", "dp", None),
            P("expert", "dp", None),
            P("expert", "dp", None),
        ),
        out_specs=(
            P(("dp", "expert"), None),
            P(("dp", "expert"), None),
            P("expert", "dp", None),
            P("expert", "dp", None),
            P("expert", "dp", None),
        ),
        check_vma=False,
    )
```

```python
import functools
import math

import jax
import jax.numpy as jnp
from jax import lax
from jax.experimental import pallas as pl
from jax.experimental.pallas import tpu as pltpu
from jax.sharding import PartitionSpec as P

F32 = jnp.float32
BF16 = jnp.bfloat16
MIB = 1024 * 1024
TILE = 8
PANEL = 256
CHUNKS = 4


def in_vmem(x):
    return pltpu.with_memory_space_constraint(x, pltpu.VMEM)


def in_hbm(x):
    return pltpu.with_memory_space_constraint(x, pltpu.HBM)


def vmem_result(*shape):
    return pltpu.VMEM(shape, BF16)


def hbm_result(*shape):
    return pltpu.HBM(shape, BF16)


def dot(a, b, ca, cb):
    return lax.dot_general(a, b, (((ca,), (cb,)), ((), ())), preferred_element_type=F32)


def split_high_low(x):
    high = x.astype(BF16)
    return high, (x - high.astype(F32)).astype(BF16)


def expert_of_row(shape, members):
    row = lax.broadcasted_iota(jnp.int32, shape, 0)
    per_member = shape[0] // members
    return lax.rem(row, per_member) * members + row // per_member


def weight_copies(gate_ref, up_ref, down_ref, packed_buf, sems):
    share = gate_ref.shape[1]
    half = share // 2
    hidden_width = gate_ref.shape[2]
    pieces = (
        (gate_ref, 0, share),
        (up_ref, share, share),
        (down_ref.at[:, :, :hidden_width], 2 * share, half),
        (down_ref.at[:, :, hidden_width:], 2 * share + half, half),
    )
    return [
        pltpu.make_async_copy(ref, packed_buf.at[:, start : start + size, :], sems.at[k])
        for k, (ref, start, size) in enumerate(pieces)
    ]


def dispatch_kernel(
    members,
    ids_ref,
    gates_ref,
    tokens_ref,
    grads_ref,
    w_gate_ref,
    w_up_ref,
    w_down_ref,
    send_ref,
    slots_ref,
    packed_ref,
    tokens_buf,
    grads_buf,
    send_buf,
    packed_buf,
    weight_sems,
    token_sems,
    send_sems,
):
    loads = [
        pltpu.make_async_copy(tokens_ref, tokens_buf, token_sems.at[0]),
        pltpu.make_async_copy(grads_ref, grads_buf, token_sems.at[1]),
    ]
    for copy in loads:
        copy.start()
    packing = weight_copies(w_gate_ref, w_up_ref, w_down_ref, packed_buf, weight_sems)
    for copy in packing:
        copy.start()
    experts, capacity, _ = send_buf.shape
    token_count, width = tokens_buf.shape
    ids = ids_ref[...]
    expert = expert_of_row((experts, token_count), members)
    named = jnp.zeros((experts, token_count), F32)
    gates = jnp.zeros((experts, token_count), F32)
    for k in range(ids.shape[0]):
        same = ids[k : k + 1, :] == expert
        named = named + jnp.where(same, 1.0, 0.0)
        gates = gates + jnp.where(same, gates_ref[k : k + 1, :], 0.0)
    earlier = lax.broadcasted_iota(jnp.int32, (token_count, token_count), 0)
    later = lax.broadcasted_iota(jnp.int32, (token_count, token_count), 1)
    before = jnp.where(earlier < later, 1.0, 0.0).astype(BF16)
    ranks = dot(named.astype(BF16), before, 1, 0)
    keys = jnp.where(named > 0.0, ranks, -1.0)
    for copy in packing + loads:
        copy.wait()
    packed_out = pltpu.make_async_copy(packed_buf, packed_ref, weight_sems.at[len(packing)])
    packed_out.start()
    tokens = tokens_buf[...]
    grads = jnp.concatenate([grads_buf[...], grads_buf[...]], axis=0)
    block = experts // CHUNKS
    count = block * capacity
    place = lax.broadcasted_iota(jnp.int32, (block, capacity, token_count), 1).astype(F32)
    sends = []
    for i in range(CHUNKS):
        start = i * block
        hit = keys[start : start + block, None, :] == place
        slots = jnp.where(hit, 1.0, 0.0).reshape(count, token_count).astype(BF16)
        slots_ref[i * count : (i + 1) * count, :] = slots
        weighted = jnp.where(hit, gates[start : start + block, None, :], 0.0)
        high, low = split_high_low(weighted.reshape(count, token_count))
        rows = dot(slots, tokens, 1, 0)
        scaled = dot(jnp.concatenate([high, low], axis=1), grads, 1, 0)
        shape = (block, capacity, width)
        here = slice(start, start + block)
        send_buf[here, :, :width] = rows.astype(BF16).reshape(shape)
        send_buf[here, :, width:] = scaled.astype(BF16).reshape(shape)
        sends.append(
            pltpu.make_async_copy(send_buf.at[here], send_ref.at[here], send_sems.at[i])
        )
        sends[i].start()
    for copy in [packed_out] + sends:
        copy.wait()


def expert_kernel(
    core_ref,
    recv_ref,
    weights_ref,
    parts_ref,
    grads_ref,
    gate_ref,
    ins_ref,
    rows_ref,
    down_ref,
    hidden_ref,
    stage_ref,
    row_sems,
    in_sems,
    out_sems,
):
    sources, capacity, _ = rows_ref.shape
    pieces, _, depth, hidden_width = weights_ref.shape
    share = depth // 3
    half = share // 2
    slot_count = sources * capacity
    width = pieces * share
    core = core_ref[0]

    def fetch(k, target):
        return pltpu.make_async_copy(
            weights_ref.at[:, core, k * share : (k + 1) * share, :], target, in_sems.at[k]
        )

    fetches = [
        fetch(0, ins_ref.at[:, :share, :]),
        fetch(1, ins_ref.at[:, share:, :]),
        fetch(2, down_ref),
    ]
    block = sources // CHUNKS
    arrivals = [
        pltpu.make_async_copy(
            recv_ref.at[i * block : (i + 1) * block],
            rows_ref.at[i * block : (i + 1) * block],
            row_sems.at[i],
        )
        for i in range(CHUNKS)
    ]
    fetches[0].start()
    arrivals[0].start()
    fetches[1].start()
    fetches[2].start()
    fetches[0].wait()
    arrivals[0].wait()
    for copy in arrivals[1:]:
        copy.start()
    fetches[1].wait()
    fetches[2].wait()
    w_gate = ins_ref[:, :share, :].reshape(width, hidden_width)
    w_up = ins_ref[:, share:, :].reshape(width, hidden_width)
    down = jnp.concatenate(
        [
            down_ref[:, :half, :].reshape(hidden_width, hidden_width),
            down_ref[:, half:, :].reshape(hidden_width, hidden_width),
        ],
        axis=1,
    )
    count = block * capacity
    tiles = capacity // TILE
    lane = lax.broadcasted_iota(jnp.int32, (block, TILE, PANEL), 2)

    def products(i):
        here = slice(i * block, (i + 1) * block)
        rows = rows_ref[here, :, :width].reshape(count, width)
        scaled = rows_ref[here, :, width:].reshape(count, width)
        return dot(rows, w_gate, 1, 0), dot(rows, w_up, 1, 0), dot(scaled, down, 1, 1)

    def activations(i, gate_pre, up_proj, hidden_grad):
        where = slice(i * count, (i + 1) * count)
        sig = jax.nn.sigmoid(gate_pre)
        act = gate_pre * sig
        hidden = (act * up_proj).astype(BF16)
        hidden_ref[where, :] = hidden
        grads_ref[where, hidden_width:] = (hidden_grad * act).astype(BF16)
        pre_grad = hidden_grad * up_proj * (sig + act * (1.0 - sig))
        grads_ref[where, :hidden_width] = pre_grad.astype(BF16)
        gate_grad = jnp.sum(hidden.astype(F32) * hidden_grad, axis=1, keepdims=True)
        gate_grad = gate_grad.reshape(block, tiles, TILE, 1)
        tile = jnp.zeros((block, TILE, PANEL), F32)
        for n in range(tiles):
            value = jnp.broadcast_to(gate_grad[:, n], (block, TILE, PANEL))
            high, low = split_high_low(value)
            tile = jnp.where(lane == 2 * n, high.astype(F32), tile)
            tile = jnp.where(lane == 2 * n + 1, low.astype(F32), tile)
        gate_ref[i * block : (i + 1) * block] = tile.astype(BF16)

    ahead = products(0)
    for i in range(CHUNKS):
        now = ahead
        if i + 1 < CHUNKS:
            arrivals[i + 1].wait()
            ahead = products(i + 1)
        activations(i, *now)

    def store(k):
        return pltpu.make_async_copy(
            stage_ref.at[k], parts_ref.at[:, k * share : (k + 1) * share, :], out_sems.at[k]
        )

    stores = [store(k) for k in range(3)]
    rows = rows_ref[:, :, :width].reshape(slot_count, width)
    for k in range(2):
        own = grads_ref[:, k * hidden_width : (k + 1) * hidden_width]
        total = dot(rows, own, 0, 0).astype(BF16)
        stage_ref[k] = total.reshape(pieces, share, hidden_width)
        stores[k].start()
    scaled = rows_ref[:, :, width:].reshape(slot_count, width)
    total = dot(hidden_ref[...], scaled, 0, 0).astype(BF16)
    stage_ref[2, :, :half, :] = total[:, :hidden_width].reshape(pieces, half, hidden_width)
    stage_ref[2, :, half:, :] = total[:, hidden_width:].reshape(pieces, half, hidden_width)
    stores[2].start()
    for copy in stores:
        copy.wait()


def input_kernel(core_ref, grads_ref, gate_ref, weights_ref, back_ref, ins_ref, sem):
    sources, panels, _, _ = back_ref.shape
    share = weights_ref.shape[2] // 3
    pieces, _, hidden_width = ins_ref.shape
    core = core_ref[0]
    load = pltpu.make_async_copy(weights_ref.at[:, core, : 2 * share, :], ins_ref, sem)
    load.start()
    back_ref[:, panels - 1] = gate_ref[...]
    load.wait()
    width = pieces * share
    w_gate = ins_ref[:, :share, :].reshape(width, hidden_width)
    w_up = ins_ref[:, share:, :].reshape(width, hidden_width)
    weights = jnp.concatenate([w_gate, w_up], axis=1)
    block = sources // CHUNKS
    count = grads_ref.shape[0] // CHUNKS
    tiles = (panels - 1) * PANEL // width
    for i in range(CHUNKS):
        here = slice(i * block, (i + 1) * block)
        grad = dot(grads_ref[i * count : (i + 1) * count, :], weights, 1, 1).astype(BF16)
        for n in range(width // PANEL):
            panel = grad[:, n * PANEL : (n + 1) * PANEL]
            back_ref[here, n * tiles : (n + 1) * tiles] = panel.reshape(block, tiles, TILE, PANEL)


def combine_kernel(members, ids_ref, gates_ref, slots_ref, back_ref, input_ref, gate_ref):
    experts, panels, _, _ = back_ref.shape
    top, token_count = ids_ref.shape
    width = input_ref.shape[1]
    slot_count = slots_ref.shape[0]
    tiles = slot_count // (experts * TILE)
    slots = slots_ref[...]
    for n in range(width // PANEL):
        rows = back_ref[:, n * tiles : (n + 1) * tiles].reshape(slot_count, PANEL)
        input_ref[:, n * PANEL : (n + 1) * PANEL] = dot(slots, rows, 0, 0).astype(BF16)
    extra = back_ref[:, panels - 1].astype(F32)
    hits = slots.astype(F32).reshape(experts, tiles * TILE, token_count)
    by_expert = jnp.zeros((experts, token_count), F32)
    for n in range(tiles):
        value = extra[:, :, 2 * n : 2 * n + 1] + extra[:, :, 2 * n + 1 : 2 * n + 2]
        picked = jnp.where(hits[:, n * TILE : (n + 1) * TILE, :] > 0.0, value, 0.0)
        by_expert = by_expert + jnp.sum(picked, axis=1)
    expert = expert_of_row((experts, token_count), members)
    ids = ids_ref[...]
    for k in range(top):
        own = jnp.where(ids[k : k + 1, :] == expert, by_expert, 0.0)
        gate_ref[k : k + 1, :] = jnp.sum(own, axis=0, keepdims=True) / gates_ref[k : k + 1, :]


def scale_kernel(scale, core_ref, sums_ref, got_ref, gate_ref, up_ref, down_ref):
    share = gate_ref.shape[1]
    half = share // 2
    hidden_width = gate_ref.shape[2]
    core = core_ref[0]

    def put(member, value):
        value = value.astype(F32) * scale
        gate_ref[member] = value[:share]
        up_ref[member] = value[share : 2 * share]
        down_ref[member, :, :hidden_width] = value[2 * share : 2 * share + half]
        down_ref[member, :, hidden_width:] = value[2 * share + half :]

    for c in range(2):

        @pl.when(core == c)
        def _(c=c):
            put(c, sums_ref[c])
            put(1 - c, got_ref[...])


def shards(tokens, out_grad, route_ids, route_gates, w_gate, w_up, w_down):
    dp_size = lax.axis_size("dp")
    expert_size = lax.axis_size("expert")
    members, share, hidden_width = w_gate.shape
    experts = members * expert_size
    chips = dp_size // members
    depth = 3 * share
    token_count, top = route_ids.shape
    width = tokens.shape[1]
    capacity = 5 * token_count * top // (4 * experts)
    slot_count = experts * capacity
    scale = 1.0 / math.sqrt(token_count * dp_size * top / members)
    params = lambda mib: pltpu.CompilerParams(vmem_limit_bytes=mib * MIB)
    vmem = pl.BlockSpec(memory_space=pltpu.VMEM)
    smem = pl.BlockSpec(memory_space=pltpu.SMEM)
    anywhere = pl.BlockSpec(memory_space=pl.ANY)

    core = lax.rem(lax.axis_index("dp"), members).astype(jnp.int32).reshape(1)
    first = core[0] == 0
    ids, core, first = lax.optimization_barrier((route_ids.T, core, first))
    gates = route_gates.T
    send, slots, packed = pl.pallas_call(
        functools.partial(dispatch_kernel, members),
        in_specs=[vmem, vmem] + [anywhere] * 5,
        out_specs=(anywhere, vmem, anywhere),
        out_shape=(
            hbm_result(experts, capacity, 2 * width),
            vmem_result(slot_count, token_count),
            hbm_result(members, depth, hidden_width),
        ),
        scratch_shapes=[
            pltpu.VMEM((token_count, width), BF16),
            pltpu.VMEM((token_count, width), BF16),
            pltpu.VMEM((experts, capacity, 2 * width), BF16),
            pltpu.VMEM((members, depth, hidden_width), BF16),
            pltpu.SemaphoreType.DMA((5,)),
            pltpu.SemaphoreType.DMA((2,)),
            pltpu.SemaphoreType.DMA((CHUNKS,)),
        ],
        compiler_params=params(24),
        name="dispatch",
    )(in_hbm(ids), in_hbm(gates), *map(in_hbm, (tokens, out_grad, w_gate, w_up, w_down)))
    weights = lax.all_gather(packed, "dp", axis=0, tiled=False)

    chip_plane = [
        [(chip * members + c) * expert_size + e for c in range(members) for e in range(expert_size)]
        for chip in range(chips)
    ]

    def exchange(x):
        return lax.all_to_all(
            x,
            ("dp", "expert"),
            split_axis=0,
            concat_axis=0,
            tiled=True,
            axis_index_groups=chip_plane,
        )

    recv = exchange(send)

    parts, row_grads, gate_tiles = pl.pallas_call(
        expert_kernel,
        in_specs=[smem, anywhere, anywhere],
        out_specs=(anywhere, vmem, vmem),
        out_shape=(
            hbm_result(dp_size, depth, hidden_width),
            vmem_result(slot_count, 2 * hidden_width),
            vmem_result(experts, TILE, PANEL),
        ),
        scratch_shapes=[
            pltpu.VMEM((dp_size, 2 * share, hidden_width), BF16),
            pltpu.VMEM((experts, capacity, 2 * width), BF16),
            pltpu.VMEM((dp_size, share, hidden_width), BF16),
            pltpu.VMEM((slot_count, hidden_width), BF16),
            pltpu.VMEM((3, dp_size, share, hidden_width), BF16),
            pltpu.SemaphoreType.DMA((CHUNKS,)),
            pltpu.SemaphoreType.DMA((3,)),
            pltpu.SemaphoreType.DMA((3,)),
        ],
        compiler_params=params(40),
        name="expert",
    )(core, in_hbm(recv), in_hbm(weights))
    same_core = [list(range(c, dp_size, members)) for c in range(members)]
    sums = lax.psum_scatter(
        parts.reshape(chips, members, depth, hidden_width),
        "dp",
        scatter_dimension=0,
        tiled=False,
        axis_index_groups=same_core,
    )

    panels = capacity * width // (TILE * PANEL) + 1
    back = pl.pallas_call(
        input_kernel,
        in_specs=[smem, vmem, vmem, anywhere],
        out_specs=vmem,
        out_shape=vmem_result(experts, panels, TILE, PANEL),
        scratch_shapes=[
            pltpu.VMEM((dp_size, 2 * share, hidden_width), BF16),
            pltpu.SemaphoreType.DMA,
        ],
        compiler_params=params(24),
        name="inputs",
    )(core, in_vmem(row_grads), in_vmem(gate_tiles), in_hbm(weights))
    back, sums = lax.optimization_barrier((exchange(back), sums))
    other = jnp.where(first, sums[1], sums[0])
    got = lax.ppermute(other, "dp", [(i, i ^ 1) for i in range(dp_size)])
    input_grad, gate_grad = pl.pallas_call(
        functools.partial(combine_kernel, members),
        out_shape=(
            jax.ShapeDtypeStruct((token_count, width), BF16),
            jax.ShapeDtypeStruct((top, token_count), F32),
        ),
        compiler_params=params(24),
        name="combine",
    )(ids, gates, in_vmem(slots), in_vmem(back))

    gate_sum, up_sum, down_sum = pl.pallas_call(
        functools.partial(scale_kernel, scale),
        in_specs=[smem, vmem, vmem],
        out_shape=tuple(jax.ShapeDtypeStruct(w.shape, F32) for w in (w_gate, w_up, w_down)),
        compiler_params=params(16),
        name="scale",
    )(core, sums, in_vmem(got))
    return (input_grad, gate_grad.T, gate_sum, up_sum, down_sum)


def solution(mesh):
    return jax.shard_map(
        shards,
        mesh=mesh,
        in_specs=(
            P(("dp", "expert"), None),
            P(("dp", "expert"), None),
            P(("dp", "expert"), None),
            P(("dp", "expert"), None),
            P("expert", "dp", None),
            P("expert", "dp", None),
            P("expert", "dp", None),
        ),
        out_specs=(
            P(("dp", "expert"), None),
            P(("dp", "expert"), None),
            P("expert", "dp", None),
            P("expert", "dp", None),
            P("expert", "dp", None),
        ),
        check_vma=False,
    )
```

```python
import functools
import math

import jax
import jax.numpy as jnp
from jax import lax
from jax.experimental import pallas as pl
from jax.experimental.pallas import tpu as pltpu
from jax.sharding import PartitionSpec as P

F32 = jnp.float32
BF16 = jnp.bfloat16
MIB = 1024 * 1024
TILE = 8
PANEL = 256
CHUNKS = 4


def in_vmem(x):
    return pltpu.with_memory_space_constraint(x, pltpu.VMEM)


def in_hbm(x):
    return pltpu.with_memory_space_constraint(x, pltpu.HBM)


def vmem_result(*shape):
    return pltpu.VMEM(shape, BF16)


def hbm_result(*shape):
    return pltpu.HBM(shape, BF16)


def dot(a, b, ca, cb):
    return lax.dot_general(a, b, (((ca,), (cb,)), ((), ())), preferred_element_type=F32)


def split_high_low(x):
    high = x.astype(BF16)
    return high, (x - high.astype(F32)).astype(BF16)


def weight_copies(gate_ref, up_ref, down_ref, packed_buf, sems):
    share = gate_ref.shape[1]
    half = share // 2
    hidden_width = gate_ref.shape[2]
    pieces = (
        (gate_ref, 0, share),
        (up_ref, share, share),
        (down_ref.at[:, :, :hidden_width], 2 * share, half),
        (down_ref.at[:, :, hidden_width:], 2 * share + half, half),
    )
    return [
        pltpu.make_async_copy(ref, packed_buf.at[:, start : start + size, :], sems.at[k])
        for k, (ref, start, size) in enumerate(pieces)
    ]


def dispatch_kernel(
    experts,
    ids_ref,
    gates_ref,
    tokens_ref,
    grads_ref,
    w_gate_ref,
    w_up_ref,
    w_down_ref,
    send_ref,
    slots_ref,
    packed_ref,
    tokens_buf,
    grads_buf,
    send_buf,
    packed_buf,
    weight_sems,
    token_sems,
    send_sems,
):
    loads = [
        pltpu.make_async_copy(tokens_ref, tokens_buf, token_sems.at[0]),
        pltpu.make_async_copy(grads_ref, grads_buf, token_sems.at[1]),
    ]
    for copy in loads:
        copy.start()
    packing = weight_copies(w_gate_ref, w_up_ref, w_down_ref, packed_buf, weight_sems)
    for copy in packing:
        copy.start()
    capacity = send_buf.shape[0] // experts
    token_count, width = tokens_buf.shape
    ids = ids_ref[...]
    expert = lax.broadcasted_iota(jnp.int32, (experts, token_count), 0)
    named = jnp.zeros((experts, token_count), F32)
    gates = jnp.zeros((experts, token_count), F32)
    for k in range(ids.shape[0]):
        same = ids[k : k + 1, :] == expert
        named = named + jnp.where(same, 1.0, 0.0)
        gates = gates + jnp.where(same, gates_ref[k : k + 1, :], 0.0)
    earlier = lax.broadcasted_iota(jnp.int32, (token_count, token_count), 0)
    later = lax.broadcasted_iota(jnp.int32, (token_count, token_count), 1)
    before = jnp.where(earlier < later, 1.0, 0.0).astype(BF16)
    ranks = dot(named.astype(BF16), before, 1, 0)
    keys = jnp.where(named > 0.0, ranks, -1.0)
    for copy in packing + loads:
        copy.wait()
    packed_out = pltpu.make_async_copy(packed_buf, packed_ref, weight_sems.at[len(packing)])
    packed_out.start()
    tokens = tokens_buf[...]
    grads = jnp.concatenate([grads_buf[...], grads_buf[...]], axis=0)
    block = experts // CHUNKS
    count = block * capacity
    place = lax.broadcasted_iota(jnp.int32, (block, capacity, token_count), 1).astype(F32)
    sends = []
    for i in range(CHUNKS):
        start = i * block
        hit = keys[start : start + block, None, :] == place
        slots = jnp.where(hit, 1.0, 0.0).reshape(count, token_count).astype(BF16)
        slots_ref[i * count : (i + 1) * count, :] = slots
        weighted = jnp.where(hit, gates[start : start + block, None, :], 0.0)
        high, low = split_high_low(weighted.reshape(count, token_count))
        rows = dot(slots, tokens, 1, 0)
        scaled = dot(jnp.concatenate([high, low], axis=1), grads, 1, 0)
        here = slice(i * count, (i + 1) * count)
        send_buf[here, :width] = rows.astype(BF16)
        send_buf[here, width:] = scaled.astype(BF16)
        sends.append(
            pltpu.make_async_copy(send_buf.at[here], send_ref.at[here], send_sems.at[i])
        )
        sends[i].start()
    for copy in [packed_out] + sends:
        copy.wait()


def expert_kernel(
    core_ref,
    recv_ref,
    weights_ref,
    parts_ref,
    grads_ref,
    gate_ref,
    ins_ref,
    rows_ref,
    down_ref,
    hidden_ref,
    stage_ref,
    row_sems,
    in_sems,
    out_sems,
):
    sources = gate_ref.shape[0]
    slot_count = rows_ref.shape[0]
    capacity = slot_count // sources
    pieces, _, depth, hidden_width = weights_ref.shape
    share = depth // 3
    half = share // 2
    width = pieces * share
    core = core_ref[0]

    def fetch(k, target):
        return pltpu.make_async_copy(
            weights_ref.at[:, core, k * share : (k + 1) * share, :], target, in_sems.at[k]
        )

    fetches = [
        fetch(0, ins_ref.at[:, :share, :]),
        fetch(1, ins_ref.at[:, share:, :]),
        fetch(2, down_ref),
    ]
    block = sources // CHUNKS
    count = block * capacity
    arrivals = [
        pltpu.make_async_copy(
            recv_ref.at[i * count : (i + 1) * count],
            rows_ref.at[i * count : (i + 1) * count],
            row_sems.at[i],
        )
        for i in range(CHUNKS)
    ]
    fetches[0].start()
    arrivals[0].start()
    fetches[1].start()
    fetches[2].start()
    fetches[0].wait()
    arrivals[0].wait()
    for copy in arrivals[1:]:
        copy.start()
    fetches[1].wait()
    fetches[2].wait()
    w_gate = ins_ref[:, :share, :].reshape(width, hidden_width)
    w_up = ins_ref[:, share:, :].reshape(width, hidden_width)
    down = jnp.concatenate(
        [
            down_ref[:, :half, :].reshape(hidden_width, hidden_width),
            down_ref[:, half:, :].reshape(hidden_width, hidden_width),
        ],
        axis=1,
    )
    tiles = capacity // TILE
    lane = lax.broadcasted_iota(jnp.int32, (block, TILE, PANEL), 2)

    def products(i):
        here = slice(i * count, (i + 1) * count)
        rows = rows_ref[here, :width]
        scaled = rows_ref[here, width:]
        return dot(rows, w_gate, 1, 0), dot(rows, w_up, 1, 0), dot(scaled, down, 1, 1)

    def activations(i, gate_pre, up_proj, hidden_grad):
        where = slice(i * count, (i + 1) * count)
        sig = jax.nn.sigmoid(gate_pre)
        act = gate_pre * sig
        hidden = (act * up_proj).astype(BF16)
        hidden_ref[where, :] = hidden
        grads_ref[where, hidden_width:] = (hidden_grad * act).astype(BF16)
        pre_grad = hidden_grad * up_proj * (sig + act * (1.0 - sig))
        grads_ref[where, :hidden_width] = pre_grad.astype(BF16)
        gate_grad = jnp.sum(hidden.astype(F32) * hidden_grad, axis=1, keepdims=True)
        gate_grad = gate_grad.reshape(block, tiles, TILE, 1)
        tile = jnp.zeros((block, TILE, PANEL), F32)
        for n in range(tiles):
            value = jnp.broadcast_to(gate_grad[:, n], (block, TILE, PANEL))
            high, low = split_high_low(value)
            tile = jnp.where(lane == 2 * n, high.astype(F32), tile)
            tile = jnp.where(lane == 2 * n + 1, low.astype(F32), tile)
        gate_ref[i * block : (i + 1) * block] = tile.astype(BF16)

    ahead = products(0)
    for i in range(CHUNKS):
        now = ahead
        if i + 1 < CHUNKS:
            arrivals[i + 1].wait()
            ahead = products(i + 1)
        activations(i, *now)

    def stores(k):
        return [
            pltpu.make_async_copy(
                stage_ref.at[k, c],
                parts_ref.at[:, core if c == 0 else 1 - core, k * share : (k + 1) * share, :],
                out_sems.at[k, c],
            )
            for c in range(2)
        ]

    sent = []
    rows = rows_ref[:, :width]
    for k in range(2):
        own = grads_ref[:, k * hidden_width : (k + 1) * hidden_width]
        total = dot(rows, own, 0, 0).astype(BF16)
        total = total.reshape(pieces // 2, 2, share, hidden_width)
        for c in range(2):
            stage_ref[k, c] = total[:, c]
        sent += stores(k)
        for copy in sent[-2:]:
            copy.start()
    scaled = rows_ref[:, width:]
    total = dot(hidden_ref[...], scaled, 0, 0).astype(BF16)
    for n in range(2):
        side = total[:, n * hidden_width : (n + 1) * hidden_width]
        side = side.reshape(pieces // 2, 2, half, hidden_width)
        for c in range(2):
            stage_ref[2, c, :, n * half : (n + 1) * half, :] = side[:, c]
    sent += stores(2)
    for copy in sent[-2:]:
        copy.start()
    for copy in sent:
        copy.wait()


def input_kernel(core_ref, grads_ref, gate_ref, weights_ref, back_ref, ins_ref, sem):
    sources, panels, _, _ = back_ref.shape
    share = weights_ref.shape[2] // 3
    pieces, _, hidden_width = ins_ref.shape
    core = core_ref[0]
    load = pltpu.make_async_copy(weights_ref.at[:, core, : 2 * share, :], ins_ref, sem)
    load.start()
    back_ref[:, panels - 1] = gate_ref[...]
    load.wait()
    width = pieces * share
    w_gate = ins_ref[:, :share, :].reshape(width, hidden_width)
    w_up = ins_ref[:, share:, :].reshape(width, hidden_width)
    weights = jnp.concatenate([w_gate, w_up], axis=1)
    block = sources // CHUNKS
    count = grads_ref.shape[0] // CHUNKS
    tiles = (panels - 1) * PANEL // width
    for i in range(CHUNKS):
        here = slice(i * block, (i + 1) * block)
        grad = dot(grads_ref[i * count : (i + 1) * count, :], weights, 1, 1).astype(BF16)
        for n in range(width // PANEL):
            panel = grad[:, n * PANEL : (n + 1) * PANEL]
            back_ref[here, n * tiles : (n + 1) * tiles] = panel.reshape(block, tiles, TILE, PANEL)


def combine_kernel(ids_ref, gates_ref, slots_ref, back_ref, input_ref, gate_ref):
    experts, panels, _, _ = back_ref.shape
    top, token_count = ids_ref.shape
    width = input_ref.shape[1]
    slot_count = slots_ref.shape[0]
    tiles = slot_count // (experts * TILE)
    slots = slots_ref[...]
    for n in range(width // PANEL):
        rows = back_ref[:, n * tiles : (n + 1) * tiles].reshape(slot_count, PANEL)
        input_ref[:, n * PANEL : (n + 1) * PANEL] = dot(slots, rows, 0, 0).astype(BF16)
    extra = back_ref[:, panels - 1].astype(F32)
    hits = slots.astype(F32).reshape(experts, tiles * TILE, token_count)
    by_expert = jnp.zeros((experts, token_count), F32)
    for n in range(tiles):
        value = extra[:, :, 2 * n : 2 * n + 1] + extra[:, :, 2 * n + 1 : 2 * n + 2]
        picked = jnp.where(hits[:, n * TILE : (n + 1) * TILE, :] > 0.0, value, 0.0)
        by_expert = by_expert + jnp.sum(picked, axis=1)
    expert = lax.broadcasted_iota(jnp.int32, (experts, token_count), 0)
    ids = ids_ref[...]
    for k in range(top):
        own = jnp.where(ids[k : k + 1, :] == expert, by_expert, 0.0)
        gate_ref[k : k + 1, :] = jnp.sum(own, axis=0, keepdims=True) / gates_ref[k : k + 1, :]


def scale_kernel(scale, core_ref, sums_ref, got_ref, gate_ref, up_ref, down_ref):
    share = gate_ref.shape[1]
    half = share // 2
    hidden_width = gate_ref.shape[2]
    core = core_ref[0]

    def put(member, value):
        value = (value.astype(F32) * scale)[None]
        here = pl.ds(member, 1)
        gate_ref[here] = value[:, :share]
        up_ref[here] = value[:, share : 2 * share]
        down_ref[here, :, :hidden_width] = value[:, 2 * share : 2 * share + half]
        down_ref[here, :, hidden_width:] = value[:, 2 * share + half :]

    put(core, sums_ref[0])
    put(1 - core, got_ref[...])


def shards(tokens, out_grad, route_ids, route_gates, w_gate, w_up, w_down):
    dp_size = lax.axis_size("dp")
    expert_size = lax.axis_size("expert")
    members, share, hidden_width = w_gate.shape
    experts = members * expert_size
    chips = dp_size // members
    depth = 3 * share
    token_count, top = route_ids.shape
    width = tokens.shape[1]
    capacity = 5 * token_count * top // (4 * experts)
    slot_count = experts * capacity
    scale = 1.0 / math.sqrt(token_count * dp_size * top / members)
    params = lambda mib: pltpu.CompilerParams(vmem_limit_bytes=mib * MIB)
    vmem = pl.BlockSpec(memory_space=pltpu.VMEM)
    smem = pl.BlockSpec(memory_space=pltpu.SMEM)
    anywhere = pl.BlockSpec(memory_space=pl.ANY)

    core = lax.rem(lax.axis_index("dp"), members).astype(jnp.int32).reshape(1)
    ids, core = lax.optimization_barrier((route_ids.T, core))
    gates = route_gates.T
    send, slots, packed = pl.pallas_call(
        functools.partial(dispatch_kernel, experts),
        in_specs=[vmem, vmem] + [anywhere] * 5,
        out_specs=(anywhere, vmem, anywhere),
        out_shape=(
            hbm_result(slot_count, 2 * width),
            vmem_result(slot_count, token_count),
            hbm_result(members, depth, hidden_width),
        ),
        scratch_shapes=[
            pltpu.VMEM((token_count, width), BF16),
            pltpu.VMEM((token_count, width), BF16),
            pltpu.VMEM((slot_count, 2 * width), BF16),
            pltpu.VMEM((members, depth, hidden_width), BF16),
            pltpu.SemaphoreType.DMA((5,)),
            pltpu.SemaphoreType.DMA((2,)),
            pltpu.SemaphoreType.DMA((CHUNKS,)),
        ],
        compiler_params=params(24),
        name="dispatch",
    )(in_hbm(ids), in_hbm(gates), *map(in_hbm, (tokens, out_grad, w_gate, w_up, w_down)))
    weights = lax.all_gather(packed, "dp", axis=0, tiled=False)

    chip_plane = [
        [(chip * members + c) * expert_size + e for e in range(expert_size) for c in range(members)]
        for chip in range(chips)
    ]

    def exchange(x):
        return lax.all_to_all(
            x,
            ("dp", "expert"),
            split_axis=0,
            concat_axis=0,
            tiled=True,
            axis_index_groups=chip_plane,
        )

    recv = exchange(send.reshape(experts, capacity, 2 * width)).reshape(slot_count, 2 * width)

    parts, row_grads, gate_tiles = pl.pallas_call(
        expert_kernel,
        in_specs=[smem, anywhere, anywhere],
        out_specs=(anywhere, vmem, vmem),
        out_shape=(
            hbm_result(chips, members, depth, hidden_width),
            vmem_result(slot_count, 2 * hidden_width),
            vmem_result(experts, TILE, PANEL),
        ),
        scratch_shapes=[
            pltpu.VMEM((dp_size, 2 * share, hidden_width), BF16),
            pltpu.VMEM((slot_count, 2 * width), BF16),
            pltpu.VMEM((dp_size, share, hidden_width), BF16),
            pltpu.VMEM((slot_count, hidden_width), BF16),
            pltpu.VMEM((3, members, chips, share, hidden_width), BF16),
            pltpu.SemaphoreType.DMA((CHUNKS,)),
            pltpu.SemaphoreType.DMA((3,)),
            pltpu.SemaphoreType.DMA((3, members)),
        ],
        compiler_params=params(40),
        name="expert",
    )(core, in_hbm(recv), in_hbm(weights))
    same_core = [list(range(c, dp_size, members)) for c in range(members)]
    sums = lax.psum_scatter(
        parts,
        "dp",
        scatter_dimension=0,
        tiled=False,
        axis_index_groups=same_core,
    )

    panels = capacity * width // (TILE * PANEL) + 1
    back = pl.pallas_call(
        input_kernel,
        in_specs=[smem, vmem, vmem, anywhere],
        out_specs=vmem,
        out_shape=vmem_result(experts, panels, TILE, PANEL),
        scratch_shapes=[
            pltpu.VMEM((dp_size, 2 * share, hidden_width), BF16),
            pltpu.SemaphoreType.DMA,
        ],
        compiler_params=params(24),
        name="inputs",
    )(core, in_vmem(row_grads), in_vmem(gate_tiles), in_hbm(weights))
    back, sums = lax.optimization_barrier((exchange(back), sums))
    got = lax.ppermute(sums[1], "dp", [(i, i ^ 1) for i in range(dp_size)])
    input_grad, gate_grad = pl.pallas_call(
        combine_kernel,
        out_shape=(
            jax.ShapeDtypeStruct((token_count, width), BF16),
            jax.ShapeDtypeStruct((top, token_count), F32),
        ),
        compiler_params=params(24),
        name="combine",
    )(ids, gates, in_vmem(slots), in_vmem(back))

    gate_sum, up_sum, down_sum = pl.pallas_call(
        functools.partial(scale_kernel, scale),
        in_specs=[smem, vmem, vmem],
        out_shape=tuple(jax.ShapeDtypeStruct(w.shape, F32) for w in (w_gate, w_up, w_down)),
        compiler_params=params(16),
        name="scale",
    )(core, sums, in_vmem(got))
    return (input_grad, gate_grad.T, gate_sum, up_sum, down_sum)


def solution(mesh):
    return jax.shard_map(
        shards,
        mesh=mesh,
        in_specs=(
            P(("dp", "expert"), None),
            P(("dp", "expert"), None),
            P(("dp", "expert"), None),
            P(("dp", "expert"), None),
            P("expert", "dp", None),
            P("expert", "dp", None),
            P("expert", "dp", None),
        ),
        out_specs=(
            P(("dp", "expert"), None),
            P(("dp", "expert"), None),
            P("expert", "dp", None),
            P("expert", "dp", None),
            P("expert", "dp", None),
        ),
        check_vma=False,
    )
```

```python
import functools
import math

import jax
import jax.numpy as jnp
from jax import lax
from jax.experimental import pallas as pl
from jax.experimental.pallas import tpu as pltpu
from jax.sharding import PartitionSpec as P

F32 = jnp.float32
BF16 = jnp.bfloat16
MIB = 1024 * 1024
TILE = 8
PANEL = 256
CHUNKS = 4
SEND_CHUNKS = 8


def in_vmem(x):
    return pltpu.with_memory_space_constraint(x, pltpu.VMEM)


def in_hbm(x):
    return pltpu.with_memory_space_constraint(x, pltpu.HBM)


def vmem_result(*shape):
    return pltpu.VMEM(shape, BF16)


def hbm_result(*shape):
    return pltpu.HBM(shape, BF16)


def dot(a, b, ca, cb):
    return lax.dot_general(a, b, (((ca,), (cb,)), ((), ())), preferred_element_type=F32)


def split_high_low(x):
    high = x.astype(BF16)
    return high, (x - high.astype(F32)).astype(BF16)


def weight_copies(gate_ref, up_ref, down_ref, packed_buf, sems):
    share = gate_ref.shape[1]
    half = share // 2
    hidden_width = gate_ref.shape[2]
    pieces = (
        (gate_ref, 0, share),
        (up_ref, share, share),
        (down_ref.at[:, :, :hidden_width], 2 * share, half),
        (down_ref.at[:, :, hidden_width:], 2 * share + half, half),
    )
    return [
        pltpu.make_async_copy(ref, packed_buf.at[:, start : start + size, :], sems.at[k])
        for k, (ref, start, size) in enumerate(pieces)
    ]


def dispatch_kernel(
    experts,
    ids_ref,
    gates_ref,
    tokens_ref,
    grads_ref,
    w_gate_ref,
    w_up_ref,
    w_down_ref,
    send_ref,
    slots_ref,
    packed_ref,
    tokens_buf,
    grads_buf,
    send_buf,
    packed_buf,
    weight_sems,
    token_sems,
    send_sems,
):
    loads = [
        pltpu.make_async_copy(tokens_ref, tokens_buf, token_sems.at[0]),
        pltpu.make_async_copy(grads_ref, grads_buf, token_sems.at[1]),
    ]
    for copy in loads:
        copy.start()
    packing = weight_copies(w_gate_ref, w_up_ref, w_down_ref, packed_buf, weight_sems)
    for copy in packing:
        copy.start()
    capacity = send_buf.shape[0] // experts
    token_count, width = tokens_buf.shape
    ids = ids_ref[...]
    expert = lax.broadcasted_iota(jnp.int32, (experts, token_count), 0)
    named = jnp.zeros((experts, token_count), F32)
    gates = jnp.zeros((experts, token_count), F32)
    for k in range(ids.shape[0]):
        same = ids[k : k + 1, :] == expert
        named = named + jnp.where(same, 1.0, 0.0)
        gates = gates + jnp.where(same, gates_ref[k : k + 1, :], 0.0)
    earlier = lax.broadcasted_iota(jnp.int32, (token_count, token_count), 0)
    later = lax.broadcasted_iota(jnp.int32, (token_count, token_count), 1)
    before = jnp.where(earlier < later, 1.0, 0.0).astype(BF16)
    ranks = dot(named.astype(BF16), before, 1, 0)
    keys = jnp.where(named > 0.0, ranks, -1.0)
    for copy in packing + loads:
        copy.wait()
    packed_out = pltpu.make_async_copy(packed_buf, packed_ref, weight_sems.at[len(packing)])
    packed_out.start()
    tokens = tokens_buf[...]
    grads = jnp.concatenate([grads_buf[...], grads_buf[...]], axis=0)
    block = experts // SEND_CHUNKS
    count = block * capacity
    place = lax.broadcasted_iota(jnp.int32, (block, capacity, token_count), 1).astype(F32)
    sends = []
    for i in range(SEND_CHUNKS):
        start = i * block
        hit = keys[start : start + block, None, :] == place
        slots = jnp.where(hit, 1.0, 0.0).reshape(count, token_count).astype(BF16)
        slots_ref[i * count : (i + 1) * count, :] = slots
        weighted = jnp.where(hit, gates[start : start + block, None, :], 0.0)
        high, low = split_high_low(weighted.reshape(count, token_count))
        rows = dot(slots, tokens, 1, 0)
        scaled = dot(jnp.concatenate([high, low], axis=1), grads, 1, 0)
        here = slice(i * count, (i + 1) * count)
        send_buf[here, :width] = rows.astype(BF16)
        send_buf[here, width:] = scaled.astype(BF16)
        sends.append(
            pltpu.make_async_copy(send_buf.at[here], send_ref.at[here], send_sems.at[i])
        )
        sends[i].start()
    for copy in [packed_out] + sends:
        copy.wait()


def expert_kernel(
    core_ref,
    recv_ref,
    weights_ref,
    parts_ref,
    grads_ref,
    gate_ref,
    ins_ref,
    rows_ref,
    down_ref,
    hidden_ref,
    stage_ref,
    row_sems,
    in_sems,
    out_sems,
):
    sources = gate_ref.shape[0]
    slot_count = rows_ref.shape[0]
    capacity = slot_count // sources
    pieces, _, depth, hidden_width = weights_ref.shape
    share = depth // 3
    half = share // 2
    width = pieces * share
    core = core_ref[0]

    def fetch(k, target):
        return pltpu.make_async_copy(
            weights_ref.at[:, core, k * share : (k + 1) * share, :], target, in_sems.at[k]
        )

    fetches = [
        fetch(0, ins_ref.at[:, :share, :]),
        fetch(1, ins_ref.at[:, share:, :]),
        fetch(2, down_ref),
    ]
    block = sources // CHUNKS
    count = block * capacity
    arrivals = [
        pltpu.make_async_copy(
            recv_ref.at[i * count : (i + 1) * count],
            rows_ref.at[i * count : (i + 1) * count],
            row_sems.at[i],
        )
        for i in range(CHUNKS)
    ]
    fetches[0].start()
    arrivals[0].start()
    fetches[1].start()
    fetches[2].start()
    fetches[0].wait()
    arrivals[0].wait()
    for copy in arrivals[1:]:
        copy.start()
    fetches[1].wait()
    fetches[2].wait()
    w_gate = ins_ref[:, :share, :].reshape(width, hidden_width)
    w_up = ins_ref[:, share:, :].reshape(width, hidden_width)
    down = jnp.concatenate(
        [
            down_ref[:, :half, :].reshape(hidden_width, hidden_width),
            down_ref[:, half:, :].reshape(hidden_width, hidden_width),
        ],
        axis=1,
    )
    tiles = capacity // TILE
    lane = lax.broadcasted_iota(jnp.int32, (block, TILE, PANEL), 2)

    def products(i):
        here = slice(i * count, (i + 1) * count)
        rows = rows_ref[here, :width]
        scaled = rows_ref[here, width:]
        return dot(rows, w_gate, 1, 0), dot(rows, w_up, 1, 0), dot(scaled, down, 1, 1)

    def activations(i, gate_pre, up_proj, hidden_grad):
        where = slice(i * count, (i + 1) * count)
        sig = jax.nn.sigmoid(gate_pre)
        act = gate_pre * sig
        hidden = (act * up_proj).astype(BF16)
        hidden_ref[where, :] = hidden
        grads_ref[where, hidden_width:] = (hidden_grad * act).astype(BF16)
        pre_grad = hidden_grad * up_proj * (sig + act * (1.0 - sig))
        grads_ref[where, :hidden_width] = pre_grad.astype(BF16)
        gate_grad = jnp.sum(hidden.astype(F32) * hidden_grad, axis=1, keepdims=True)
        gate_grad = gate_grad.reshape(block, tiles, TILE, 1)
        tile = jnp.zeros((block, TILE, PANEL), F32)
        for n in range(tiles):
            value = jnp.broadcast_to(gate_grad[:, n], (block, TILE, PANEL))
            high, low = split_high_low(value)
            tile = jnp.where(lane == 2 * n, high.astype(F32), tile)
            tile = jnp.where(lane == 2 * n + 1, low.astype(F32), tile)
        gate_ref[i * block : (i + 1) * block] = tile.astype(BF16)

    ahead = products(0)
    for i in range(CHUNKS):
        now = ahead
        if i + 1 < CHUNKS:
            arrivals[i + 1].wait()
            ahead = products(i + 1)
        activations(i, *now)

    def stores(k):
        return [
            pltpu.make_async_copy(
                stage_ref.at[k, c],
                parts_ref.at[:, core if c == 0 else 1 - core, k * share : (k + 1) * share, :],
                out_sems.at[k, c],
            )
            for c in range(2)
        ]

    sent = []
    rows = rows_ref[:, :width]
    for k in range(2):
        own = grads_ref[:, k * hidden_width : (k + 1) * hidden_width]
        total = dot(rows, own, 0, 0).astype(BF16)
        total = total.reshape(pieces // 2, 2, share, hidden_width)
        for c in range(2):
            stage_ref[k, c] = total[:, c]
        sent += stores(k)
        for copy in sent[-2:]:
            copy.start()
    scaled = rows_ref[:, width:]
    total = dot(hidden_ref[...], scaled, 0, 0).astype(BF16)
    for n in range(2):
        side = total[:, n * hidden_width : (n + 1) * hidden_width]
        side = side.reshape(pieces // 2, 2, half, hidden_width)
        for c in range(2):
            stage_ref[2, c, :, n * half : (n + 1) * half, :] = side[:, c]
    sent += stores(2)
    for copy in sent[-2:]:
        copy.start()
    for copy in sent:
        copy.wait()


def input_kernel(core_ref, grads_ref, gate_ref, weights_ref, back_ref, ins_ref, sem):
    sources, panels, _, _ = back_ref.shape
    share = weights_ref.shape[2] // 3
    pieces, _, hidden_width = ins_ref.shape
    core = core_ref[0]
    load = pltpu.make_async_copy(weights_ref.at[:, core, : 2 * share, :], ins_ref, sem)
    load.start()
    back_ref[:, panels - 1] = gate_ref[...]
    load.wait()
    width = pieces * share
    w_gate = ins_ref[:, :share, :].reshape(width, hidden_width)
    w_up = ins_ref[:, share:, :].reshape(width, hidden_width)
    weights = jnp.concatenate([w_gate, w_up], axis=1)
    block = sources // CHUNKS
    count = grads_ref.shape[0] // CHUNKS
    tiles = (panels - 1) * PANEL // width
    for i in range(CHUNKS):
        here = slice(i * block, (i + 1) * block)
        grad = dot(grads_ref[i * count : (i + 1) * count, :], weights, 1, 1).astype(BF16)
        for n in range(width // PANEL):
            panel = grad[:, n * PANEL : (n + 1) * PANEL]
            back_ref[here, n * tiles : (n + 1) * tiles] = panel.reshape(block, tiles, TILE, PANEL)


def combine_kernel(ids_ref, gates_ref, slots_ref, back_ref, input_ref, gate_ref):
    experts, panels, _, _ = back_ref.shape
    top, token_count = ids_ref.shape
    width = input_ref.shape[1]
    slot_count = slots_ref.shape[0]
    tiles = slot_count // (experts * TILE)
    slots = slots_ref[...]
    for n in range(width // PANEL):
        rows = back_ref[:, n * tiles : (n + 1) * tiles].reshape(slot_count, PANEL)
        input_ref[:, n * PANEL : (n + 1) * PANEL] = dot(slots, rows, 0, 0).astype(BF16)
    extra = back_ref[:, panels - 1].astype(F32)
    hits = slots.astype(F32).reshape(experts, tiles * TILE, token_count)
    by_expert = jnp.zeros((experts, token_count), F32)
    for n in range(tiles):
        value = extra[:, :, 2 * n : 2 * n + 1] + extra[:, :, 2 * n + 1 : 2 * n + 2]
        picked = jnp.where(hits[:, n * TILE : (n + 1) * TILE, :] > 0.0, value, 0.0)
        by_expert = by_expert + jnp.sum(picked, axis=1)
    expert = lax.broadcasted_iota(jnp.int32, (experts, token_count), 0)
    ids = ids_ref[...]
    for k in range(top):
        own = jnp.where(ids[k : k + 1, :] == expert, by_expert, 0.0)
        gate_ref[k : k + 1, :] = jnp.sum(own, axis=0, keepdims=True) / gates_ref[k : k + 1, :]


def scale_kernel(scale, core_ref, sums_ref, got_ref, gate_ref, up_ref, down_ref):
    share = gate_ref.shape[1]
    half = share // 2
    hidden_width = gate_ref.shape[2]
    core = core_ref[0]

    def put(member, value):
        value = (value.astype(F32) * scale)[None]
        here = pl.ds(member, 1)
        gate_ref[here] = value[:, :share]
        up_ref[here] = value[:, share : 2 * share]
        down_ref[here, :, :hidden_width] = value[:, 2 * share : 2 * share + half]
        down_ref[here, :, hidden_width:] = value[:, 2 * share + half :]

    put(core, sums_ref[0])
    put(1 - core, got_ref[1])


def shards(tokens, out_grad, route_ids, route_gates, w_gate, w_up, w_down):
    dp_size = lax.axis_size("dp")
    expert_size = lax.axis_size("expert")
    members, share, hidden_width = w_gate.shape
    experts = members * expert_size
    chips = dp_size // members
    depth = 3 * share
    token_count, top = route_ids.shape
    width = tokens.shape[1]
    capacity = 5 * token_count * top // (4 * experts)
    slot_count = experts * capacity
    scale = 1.0 / math.sqrt(token_count * dp_size * top / members)
    params = lambda mib: pltpu.CompilerParams(vmem_limit_bytes=mib * MIB)
    vmem = pl.BlockSpec(memory_space=pltpu.VMEM)
    smem = pl.BlockSpec(memory_space=pltpu.SMEM)
    anywhere = pl.BlockSpec(memory_space=pl.ANY)

    core = lax.rem(lax.axis_index("dp"), members).astype(jnp.int32).reshape(1)
    ids, core = lax.optimization_barrier((route_ids.T, core))
    gates = route_gates.T
    send, slots, packed = pl.pallas_call(
        functools.partial(dispatch_kernel, experts),
        in_specs=[vmem, vmem] + [anywhere] * 5,
        out_specs=(anywhere, vmem, anywhere),
        out_shape=(
            hbm_result(slot_count, 2 * width),
            vmem_result(slot_count, token_count),
            hbm_result(members, depth, hidden_width),
        ),
        scratch_shapes=[
            pltpu.VMEM((token_count, width), BF16),
            pltpu.VMEM((token_count, width), BF16),
            pltpu.VMEM((slot_count, 2 * width), BF16),
            pltpu.VMEM((members, depth, hidden_width), BF16),
            pltpu.SemaphoreType.DMA((5,)),
            pltpu.SemaphoreType.DMA((2,)),
            pltpu.SemaphoreType.DMA((SEND_CHUNKS,)),
        ],
        compiler_params=params(24),
        name="dispatch",
    )(in_hbm(ids), in_hbm(gates), *map(in_hbm, (tokens, out_grad, w_gate, w_up, w_down)))
    weights = lax.all_gather(packed, "dp", axis=0, tiled=False)

    chip_plane = [
        [(chip * members + c) * expert_size + e for e in range(expert_size) for c in range(members)]
        for chip in range(chips)
    ]

    def exchange(x):
        return lax.all_to_all(
            x,
            ("dp", "expert"),
            split_axis=0,
            concat_axis=0,
            tiled=True,
            axis_index_groups=chip_plane,
        )

    recv = exchange(send.reshape(experts, capacity, 2 * width)).reshape(slot_count, 2 * width)

    parts, row_grads, gate_tiles = pl.pallas_call(
        expert_kernel,
        in_specs=[smem, anywhere, anywhere],
        out_specs=(anywhere, vmem, vmem),
        out_shape=(
            hbm_result(chips, members, depth, hidden_width),
            vmem_result(slot_count, 2 * hidden_width),
            vmem_result(experts, TILE, PANEL),
        ),
        scratch_shapes=[
            pltpu.VMEM((dp_size, 2 * share, hidden_width), BF16),
            pltpu.VMEM((slot_count, 2 * width), BF16),
            pltpu.VMEM((dp_size, share, hidden_width), BF16),
            pltpu.VMEM((slot_count, hidden_width), BF16),
            pltpu.VMEM((3, members, chips, share, hidden_width), BF16),
            pltpu.SemaphoreType.DMA((CHUNKS,)),
            pltpu.SemaphoreType.DMA((3,)),
            pltpu.SemaphoreType.DMA((3, members)),
        ],
        compiler_params=params(40),
        name="expert",
    )(core, in_hbm(recv), in_hbm(weights))
    same_core = [list(range(c, dp_size, members)) for c in range(members)]
    sums = lax.psum_scatter(
        parts,
        "dp",
        scatter_dimension=0,
        tiled=False,
        axis_index_groups=same_core,
    )

    panels = capacity * width // (TILE * PANEL) + 1
    back = pl.pallas_call(
        input_kernel,
        in_specs=[smem, vmem, vmem, anywhere],
        out_specs=vmem,
        out_shape=vmem_result(experts, panels, TILE, PANEL),
        scratch_shapes=[
            pltpu.VMEM((dp_size, 2 * share, hidden_width), BF16),
            pltpu.SemaphoreType.DMA,
        ],
        compiler_params=params(24),
        name="inputs",
    )(core, in_vmem(row_grads), in_vmem(gate_tiles), in_hbm(weights))
    back, sums = lax.optimization_barrier((exchange(back), sums))
    got = lax.ppermute(sums, "dp", [(i, i ^ 1) for i in range(dp_size)])
    input_grad, gate_grad = pl.pallas_call(
        combine_kernel,
        out_shape=(
            jax.ShapeDtypeStruct((token_count, width), BF16),
            jax.ShapeDtypeStruct((top, token_count), F32),
        ),
        compiler_params=params(24),
        name="combine",
    )(ids, gates, in_vmem(slots), in_vmem(back))

    gate_sum, up_sum, down_sum = pl.pallas_call(
        functools.partial(scale_kernel, scale),
        in_specs=[smem, vmem, vmem],
        out_shape=tuple(jax.ShapeDtypeStruct(w.shape, F32) for w in (w_gate, w_up, w_down)),
        compiler_params=params(16),
        name="scale",
    )(core, sums, in_vmem(got))
    return (input_grad, gate_grad.T, gate_sum, up_sum, down_sum)


def solution(mesh):
    return jax.shard_map(
        shards,
        mesh=mesh,
        in_specs=(
            P(("dp", "expert"), None),
            P(("dp", "expert"), None),
            P(("dp", "expert"), None),
            P(("dp", "expert"), None),
            P("expert", "dp", None),
            P("expert", "dp", None),
            P("expert", "dp", None),
        ),
        out_specs=(
            P(("dp", "expert"), None),
            P(("dp", "expert"), None),
            P("expert", "dp", None),
            P("expert", "dp", None),
            P("expert", "dp", None),
        ),
        check_vma=False,
    )
```

```python
import functools
import math

import jax
import jax.numpy as jnp
from jax import lax
from jax.experimental import pallas as pl
from jax.experimental.pallas import tpu as pltpu
from jax.sharding import PartitionSpec as P

F32 = jnp.float32
BF16 = jnp.bfloat16
MIB = 1024 * 1024
TILE = 8
PANEL = 256
CHUNKS = 4
SEND_CHUNKS = 8


def in_vmem(x):
    return pltpu.with_memory_space_constraint(x, pltpu.VMEM)


def in_hbm(x):
    return pltpu.with_memory_space_constraint(x, pltpu.HBM)


def vmem_result(*shape):
    return pltpu.VMEM(shape, BF16)


def hbm_result(*shape):
    return pltpu.HBM(shape, BF16)


def dot(a, b, ca, cb):
    return lax.dot_general(a, b, (((ca,), (cb,)), ((), ())), preferred_element_type=F32)


def split_high_low(x):
    high = x.astype(BF16)
    return high, (x - high.astype(F32)).astype(BF16)


def expert_of_row(shape, members):
    row = lax.broadcasted_iota(jnp.int32, shape, 0)
    per_member = shape[0] // members
    return lax.rem(row, per_member) * members + row // per_member


def weight_copies(gate_ref, up_ref, down_ref, packed_buf, sems):
    share = gate_ref.shape[1]
    half = share // 2
    hidden_width = gate_ref.shape[2]
    pieces = (
        (gate_ref, 0, share),
        (up_ref, share, share),
        (down_ref.at[:, :, :hidden_width], 2 * share, half),
        (down_ref.at[:, :, hidden_width:], 2 * share + half, half),
    )
    return [
        pltpu.make_async_copy(ref, packed_buf.at[:, start : start + size, :], sems.at[k])
        for k, (ref, start, size) in enumerate(pieces)
    ]


def dispatch_kernel(
    members,
    experts,
    ids_ref,
    gates_ref,
    tokens_ref,
    grads_ref,
    w_gate_ref,
    w_up_ref,
    w_down_ref,
    send_ref,
    slots_ref,
    packed_ref,
    tokens_buf,
    grads_buf,
    send_buf,
    packed_buf,
    weight_sems,
    token_sems,
    send_sems,
):
    loads = [
        pltpu.make_async_copy(tokens_ref, tokens_buf, token_sems.at[0]),
        pltpu.make_async_copy(grads_ref, grads_buf, token_sems.at[1]),
    ]
    for copy in loads:
        copy.start()
    packing = weight_copies(w_gate_ref, w_up_ref, w_down_ref, packed_buf, weight_sems)
    for copy in packing:
        copy.start()
    capacity = send_buf.shape[0] // experts
    token_count, width = tokens_buf.shape
    ids = ids_ref[...]
    expert = expert_of_row((experts, token_count), members)
    named = jnp.zeros((experts, token_count), F32)
    gates = jnp.zeros((experts, token_count), F32)
    for k in range(ids.shape[0]):
        same = ids[k : k + 1, :] == expert
        named = named + jnp.where(same, 1.0, 0.0)
        gates = gates + jnp.where(same, gates_ref[k : k + 1, :], 0.0)
    earlier = lax.broadcasted_iota(jnp.int32, (token_count, token_count), 0)
    later = lax.broadcasted_iota(jnp.int32, (token_count, token_count), 1)
    before = jnp.where(earlier < later, 1.0, 0.0).astype(BF16)
    ranks = dot(named.astype(BF16), before, 1, 0)
    keys = jnp.where(named > 0.0, ranks, -1.0)
    for copy in packing + loads:
        copy.wait()
    packed_out = pltpu.make_async_copy(packed_buf, packed_ref, weight_sems.at[len(packing)])
    packed_out.start()
    tokens = tokens_buf[...]
    grads = jnp.concatenate([grads_buf[...], grads_buf[...]], axis=0)
    block = experts // SEND_CHUNKS
    count = block * capacity
    place = lax.broadcasted_iota(jnp.int32, (block, capacity, token_count), 1).astype(F32)
    sends = []
    for i in range(SEND_CHUNKS):
        start = i * block
        hit = keys[start : start + block, None, :] == place
        slots = jnp.where(hit, 1.0, 0.0).reshape(count, token_count).astype(BF16)
        slots_ref[i * count : (i + 1) * count, :] = slots
        weighted = jnp.where(hit, gates[start : start + block, None, :], 0.0)
        high, low = split_high_low(weighted.reshape(count, token_count))
        rows = dot(slots, tokens, 1, 0)
        scaled = dot(jnp.concatenate([high, low], axis=1), grads, 1, 0)
        here = slice(i * count, (i + 1) * count)
        send_buf[here, :width] = rows.astype(BF16)
        send_buf[here, width:] = scaled.astype(BF16)
        sends.append(
            pltpu.make_async_copy(send_buf.at[here], send_ref.at[here], send_sems.at[i])
        )
        sends[i].start()
    for copy in [packed_out] + sends:
        copy.wait()


def expert_kernel(
    core_ref,
    recv_ref,
    weights_ref,
    parts_ref,
    grads_ref,
    gate_ref,
    ins_ref,
    rows_ref,
    down_ref,
    hidden_ref,
    stage_ref,
    row_sems,
    in_sems,
    out_sems,
):
    sources = gate_ref.shape[0]
    slot_count = rows_ref.shape[0]
    capacity = slot_count // sources
    pieces, _, depth, hidden_width = weights_ref.shape
    share = depth // 3
    half = share // 2
    width = pieces * share
    core = core_ref[0]

    def fetch(k, target):
        return pltpu.make_async_copy(
            weights_ref.at[:, core, k * share : (k + 1) * share, :], target, in_sems.at[k]
        )

    fetches = [
        fetch(0, ins_ref.at[:, :share, :]),
        fetch(1, ins_ref.at[:, share:, :]),
        fetch(2, down_ref),
    ]
    block = sources // CHUNKS
    count = block * capacity
    arrivals = [
        pltpu.make_async_copy(
            recv_ref.at[i * count : (i + 1) * count],
            rows_ref.at[i * count : (i + 1) * count],
            row_sems.at[i],
        )
        for i in range(CHUNKS)
    ]
    fetches[0].start()
    arrivals[0].start()
    fetches[1].start()
    fetches[2].start()
    fetches[0].wait()
    arrivals[0].wait()
    for copy in arrivals[1:]:
        copy.start()
    fetches[1].wait()
    fetches[2].wait()
    w_gate = ins_ref[:, :share, :].reshape(width, hidden_width)
    w_up = ins_ref[:, share:, :].reshape(width, hidden_width)
    down = jnp.concatenate(
        [
            down_ref[:, :half, :].reshape(hidden_width, hidden_width),
            down_ref[:, half:, :].reshape(hidden_width, hidden_width),
        ],
        axis=1,
    )
    tiles = capacity // TILE
    lane = lax.broadcasted_iota(jnp.int32, (block, TILE, PANEL), 2)

    def products(i):
        here = slice(i * count, (i + 1) * count)
        rows = rows_ref[here, :width]
        scaled = rows_ref[here, width:]
        return dot(rows, w_gate, 1, 0), dot(rows, w_up, 1, 0), dot(scaled, down, 1, 1)

    def activations(i, gate_pre, up_proj, hidden_grad):
        where = slice(i * count, (i + 1) * count)
        sig = jax.nn.sigmoid(gate_pre)
        act = gate_pre * sig
        hidden = (act * up_proj).astype(BF16)
        hidden_ref[where, :] = hidden
        grads_ref[where, hidden_width:] = (hidden_grad * act).astype(BF16)
        pre_grad = hidden_grad * up_proj * (sig + act * (1.0 - sig))
        grads_ref[where, :hidden_width] = pre_grad.astype(BF16)
        gate_grad = jnp.sum(hidden.astype(F32) * hidden_grad, axis=1, keepdims=True)
        gate_grad = gate_grad.reshape(block, tiles, TILE, 1)
        tile = jnp.zeros((block, TILE, PANEL), F32)
        for n in range(tiles):
            value = jnp.broadcast_to(gate_grad[:, n], (block, TILE, PANEL))
            high, low = split_high_low(value)
            tile = jnp.where(lane == 2 * n, high.astype(F32), tile)
            tile = jnp.where(lane == 2 * n + 1, low.astype(F32), tile)
        gate_ref[i * block : (i + 1) * block] = tile.astype(BF16)

    ahead = products(0)
    for i in range(CHUNKS):
        now = ahead
        if i + 1 < CHUNKS:
            arrivals[i + 1].wait()
            ahead = products(i + 1)
        activations(i, *now)

    def stores(k):
        return [
            pltpu.make_async_copy(
                stage_ref.at[k, c],
                parts_ref.at[:, core if c == 0 else 1 - core, k * share : (k + 1) * share, :],
                out_sems.at[k, c],
            )
            for c in range(2)
        ]

    sent = []
    rows = rows_ref[:, :width]
    for k in range(2):
        own = grads_ref[:, k * hidden_width : (k + 1) * hidden_width]
        total = dot(rows, own, 0, 0).astype(BF16)
        total = total.reshape(pieces // 2, 2, share, hidden_width)
        for c in range(2):
            stage_ref[k, c] = total[:, c]
        sent += stores(k)
        for copy in sent[-2:]:
            copy.start()
    scaled = rows_ref[:, width:]
    total = dot(hidden_ref[...], scaled, 0, 0).astype(BF16)
    for n in range(2):
        side = total[:, n * hidden_width : (n + 1) * hidden_width]
        side = side.reshape(pieces // 2, 2, half, hidden_width)
        for c in range(2):
            stage_ref[2, c, :, n * half : (n + 1) * half, :] = side[:, c]
    sent += stores(2)
    for copy in sent[-2:]:
        copy.start()
    for copy in sent:
        copy.wait()


def input_kernel(core_ref, grads_ref, gate_ref, weights_ref, back_ref, ins_ref, sem):
    sources, panels, _, _ = back_ref.shape
    share = weights_ref.shape[2] // 3
    pieces, _, hidden_width = ins_ref.shape
    core = core_ref[0]
    load = pltpu.make_async_copy(weights_ref.at[:, core, : 2 * share, :], ins_ref, sem)
    load.start()
    back_ref[:, panels - 1] = gate_ref[...]
    load.wait()
    width = pieces * share
    w_gate = ins_ref[:, :share, :].reshape(width, hidden_width)
    w_up = ins_ref[:, share:, :].reshape(width, hidden_width)
    weights = jnp.concatenate([w_gate, w_up], axis=1)
    block = sources // CHUNKS
    count = grads_ref.shape[0] // CHUNKS
    tiles = (panels - 1) * PANEL // width
    for i in range(CHUNKS):
        here = slice(i * block, (i + 1) * block)
        grad = dot(grads_ref[i * count : (i + 1) * count, :], weights, 1, 1).astype(BF16)
        for n in range(width // PANEL):
            panel = grad[:, n * PANEL : (n + 1) * PANEL]
            back_ref[here, n * tiles : (n + 1) * tiles] = panel.reshape(block, tiles, TILE, PANEL)


def combine_kernel(members, ids_ref, gates_ref, slots_ref, back_ref, input_ref, gate_ref):
    experts, panels, _, _ = back_ref.shape
    top, token_count = ids_ref.shape
    width = input_ref.shape[1]
    slot_count = slots_ref.shape[0]
    tiles = slot_count // (experts * TILE)
    slots = slots_ref[...]
    for n in range(width // PANEL):
        rows = back_ref[:, n * tiles : (n + 1) * tiles].reshape(slot_count, PANEL)
        input_ref[:, n * PANEL : (n + 1) * PANEL] = dot(slots, rows, 0, 0).astype(BF16)
    extra = back_ref[:, panels - 1].astype(F32)
    hits = slots.astype(F32).reshape(experts, tiles * TILE, token_count)
    by_expert = jnp.zeros((experts, token_count), F32)
    for n in range(tiles):
        value = extra[:, :, 2 * n : 2 * n + 1] + extra[:, :, 2 * n + 1 : 2 * n + 2]
        picked = jnp.where(hits[:, n * TILE : (n + 1) * TILE, :] > 0.0, value, 0.0)
        by_expert = by_expert + jnp.sum(picked, axis=1)
    expert = expert_of_row((experts, token_count), members)
    ids = ids_ref[...]
    for k in range(top):
        own = jnp.where(ids[k : k + 1, :] == expert, by_expert, 0.0)
        gate_ref[k : k + 1, :] = jnp.sum(own, axis=0, keepdims=True) / gates_ref[k : k + 1, :]


def scale_kernel(scale, core_ref, sums_ref, got_ref, gate_ref, up_ref, down_ref):
    share = gate_ref.shape[1]
    half = share // 2
    hidden_width = gate_ref.shape[2]
    core = core_ref[0]

    def put(member, value):
        value = (value.astype(F32) * scale)[None]
        here = pl.ds(member, 1)
        gate_ref[here] = value[:, :share]
        up_ref[here] = value[:, share : 2 * share]
        down_ref[here, :, :hidden_width] = value[:, 2 * share : 2 * share + half]
        down_ref[here, :, hidden_width:] = value[:, 2 * share + half :]

    put(core, sums_ref[0])
    put(1 - core, got_ref[1])


def shards(tokens, out_grad, route_ids, route_gates, w_gate, w_up, w_down):
    dp_size = lax.axis_size("dp")
    expert_size = lax.axis_size("expert")
    members, share, hidden_width = w_gate.shape
    experts = members * expert_size
    chips = dp_size // members
    depth = 3 * share
    token_count, top = route_ids.shape
    width = tokens.shape[1]
    capacity = 5 * token_count * top // (4 * experts)
    slot_count = experts * capacity
    scale = 1.0 / math.sqrt(token_count * dp_size * top / members)
    params = lambda mib: pltpu.CompilerParams(vmem_limit_bytes=mib * MIB)
    vmem = pl.BlockSpec(memory_space=pltpu.VMEM)
    smem = pl.BlockSpec(memory_space=pltpu.SMEM)
    anywhere = pl.BlockSpec(memory_space=pl.ANY)

    core = lax.rem(lax.axis_index("dp"), members).astype(jnp.int32).reshape(1)
    ids, core = lax.optimization_barrier((route_ids.T, core))
    gates = route_gates.T
    send, slots, packed = pl.pallas_call(
        functools.partial(dispatch_kernel, members, experts),
        in_specs=[vmem, vmem] + [anywhere] * 5,
        out_specs=(anywhere, vmem, anywhere),
        out_shape=(
            hbm_result(slot_count, 2 * width),
            vmem_result(slot_count, token_count),
            hbm_result(members, depth, hidden_width),
        ),
        scratch_shapes=[
            pltpu.VMEM((token_count, width), BF16),
            pltpu.VMEM((token_count, width), BF16),
            pltpu.VMEM((slot_count, 2 * width), BF16),
            pltpu.VMEM((members, depth, hidden_width), BF16),
            pltpu.SemaphoreType.DMA((5,)),
            pltpu.SemaphoreType.DMA((2,)),
            pltpu.SemaphoreType.DMA((SEND_CHUNKS,)),
        ],
        compiler_params=params(24),
        name="dispatch",
    )(in_hbm(ids), in_hbm(gates), *map(in_hbm, (tokens, out_grad, w_gate, w_up, w_down)))
    weights = lax.all_gather(packed, "dp", axis=0, tiled=False)

    chip_plane = [
        [(chip * members + c) * expert_size + e for c in range(members) for e in range(expert_size)]
        for chip in range(chips)
    ]

    def exchange(x):
        return lax.all_to_all(
            x,
            ("dp", "expert"),
            split_axis=0,
            concat_axis=0,
            tiled=True,
            axis_index_groups=chip_plane,
        )

    recv = exchange(send.reshape(experts, capacity, 2 * width)).reshape(slot_count, 2 * width)

    parts, row_grads, gate_tiles = pl.pallas_call(
        expert_kernel,
        in_specs=[smem, anywhere, anywhere],
        out_specs=(anywhere, vmem, vmem),
        out_shape=(
            hbm_result(chips, members, depth, hidden_width),
            vmem_result(slot_count, 2 * hidden_width),
            vmem_result(experts, TILE, PANEL),
        ),
        scratch_shapes=[
            pltpu.VMEM((dp_size, 2 * share, hidden_width), BF16),
            pltpu.VMEM((slot_count, 2 * width), BF16),
            pltpu.VMEM((dp_size, share, hidden_width), BF16),
            pltpu.VMEM((slot_count, hidden_width), BF16),
            pltpu.VMEM((3, members, chips, share, hidden_width), BF16),
            pltpu.SemaphoreType.DMA((CHUNKS,)),
            pltpu.SemaphoreType.DMA((3,)),
            pltpu.SemaphoreType.DMA((3, members)),
        ],
        compiler_params=params(40),
        name="expert",
    )(core, in_hbm(recv), in_hbm(weights))
    same_core = [list(range(c, dp_size, members)) for c in range(members)]
    sums = lax.psum_scatter(
        parts,
        "dp",
        scatter_dimension=0,
        tiled=False,
        axis_index_groups=same_core,
    )

    panels = capacity * width // (TILE * PANEL) + 1
    back = pl.pallas_call(
        input_kernel,
        in_specs=[smem, vmem, vmem, anywhere],
        out_specs=vmem,
        out_shape=vmem_result(experts, panels, TILE, PANEL),
        scratch_shapes=[
            pltpu.VMEM((dp_size, 2 * share, hidden_width), BF16),
            pltpu.SemaphoreType.DMA,
        ],
        compiler_params=params(24),
        name="inputs",
    )(core, in_vmem(row_grads), in_vmem(gate_tiles), in_hbm(weights))
    back, sums = lax.optimization_barrier((exchange(back), sums))
    got = lax.ppermute(sums, "dp", [(i, i ^ 1) for i in range(dp_size)])
    input_grad, gate_grad = pl.pallas_call(
        functools.partial(combine_kernel, members),
        out_shape=(
            jax.ShapeDtypeStruct((token_count, width), BF16),
            jax.ShapeDtypeStruct((top, token_count), F32),
        ),
        compiler_params=params(24),
        name="combine",
    )(ids, gates, in_vmem(slots), in_vmem(back))

    gate_sum, up_sum, down_sum = pl.pallas_call(
        functools.partial(scale_kernel, scale),
        in_specs=[smem, vmem, vmem],
        out_shape=tuple(jax.ShapeDtypeStruct(w.shape, F32) for w in (w_gate, w_up, w_down)),
        compiler_params=params(16),
        name="scale",
    )(core, sums, in_vmem(got))
    return (input_grad, gate_grad.T, gate_sum, up_sum, down_sum)


def solution(mesh):
    return jax.shard_map(
        shards,
        mesh=mesh,
        in_specs=(
            P(("dp", "expert"), None),
            P(("dp", "expert"), None),
            P(("dp", "expert"), None),
            P(("dp", "expert"), None),
            P("expert", "dp", None),
            P("expert", "dp", None),
            P("expert", "dp", None),
        ),
        out_specs=(
            P(("dp", "expert"), None),
            P(("dp", "expert"), None),
            P("expert", "dp", None),
            P("expert", "dp", None),
            P("expert", "dp", None),
        ),
        check_vma=False,
    )
```

```python
import functools
import math

import jax
import jax.numpy as jnp
from jax import lax
from jax.experimental import pallas as pl
from jax.experimental.pallas import tpu as pltpu
from jax.sharding import PartitionSpec as P

F32 = jnp.float32
BF16 = jnp.bfloat16
MIB = 1024 * 1024
TILE = 8
PANEL = 256
CHUNKS = 4
SEND_CHUNKS = 8


def in_vmem(x):
    return pltpu.with_memory_space_constraint(x, pltpu.VMEM)


def in_hbm(x):
    return pltpu.with_memory_space_constraint(x, pltpu.HBM)


def vmem_result(*shape):
    return pltpu.VMEM(shape, BF16)


def hbm_result(*shape):
    return pltpu.HBM(shape, BF16)


def dot(a, b, ca, cb):
    return lax.dot_general(a, b, (((ca,), (cb,)), ((), ())), preferred_element_type=F32)


def split_high_low(x):
    high = x.astype(BF16)
    return high, (x - high.astype(F32)).astype(BF16)


def expert_of_row(shape, members):
    row = lax.broadcasted_iota(jnp.int32, shape, 0)
    per_member = shape[0] // members
    return lax.rem(row, per_member) * members + row // per_member


def weight_copies(gate_ref, up_ref, down_ref, packed_buf, sems):
    share = gate_ref.shape[1]
    half = share // 2
    hidden_width = gate_ref.shape[2]
    pieces = (
        (gate_ref, 0, share),
        (up_ref, share, share),
        (down_ref.at[:, :, :hidden_width], 2 * share, half),
        (down_ref.at[:, :, hidden_width:], 2 * share + half, half),
    )
    return [
        pltpu.make_async_copy(ref, packed_buf.at[:, start : start + size, :], sems.at[k])
        for k, (ref, start, size) in enumerate(pieces)
    ]


def dispatch_kernel(
    members,
    experts,
    ids_ref,
    gates_ref,
    tokens_ref,
    grads_ref,
    w_gate_ref,
    w_up_ref,
    w_down_ref,
    send_ref,
    slots_ref,
    packed_ref,
    tokens_buf,
    grads_buf,
    send_buf,
    packed_buf,
    weight_sems,
    token_sems,
    send_sems,
):
    loads = [
        pltpu.make_async_copy(tokens_ref, tokens_buf, token_sems.at[0]),
        pltpu.make_async_copy(grads_ref, grads_buf, token_sems.at[1]),
    ]
    for copy in loads:
        copy.start()
    packing = weight_copies(w_gate_ref, w_up_ref, w_down_ref, packed_buf, weight_sems)
    for copy in packing:
        copy.start()
    capacity = send_buf.shape[0] // experts
    token_count, width = tokens_buf.shape
    ids = ids_ref[...]
    expert = expert_of_row((experts, token_count), members)
    named = jnp.zeros((experts, token_count), F32)
    gates = jnp.zeros((experts, token_count), F32)
    for k in range(ids.shape[0]):
        same = ids[k : k + 1, :] == expert
        named = named + jnp.where(same, 1.0, 0.0)
        gates = gates + jnp.where(same, gates_ref[k : k + 1, :], 0.0)
    earlier = lax.broadcasted_iota(jnp.int32, (token_count, token_count), 0)
    later = lax.broadcasted_iota(jnp.int32, (token_count, token_count), 1)
    before = jnp.where(earlier < later, 1.0, 0.0).astype(BF16)
    ranks = dot(named.astype(BF16), before, 1, 0)
    keys = jnp.where(named > 0.0, ranks, -1.0)
    for copy in loads:
        copy.wait()
    tokens = tokens_buf[...]
    grads = jnp.concatenate([grads_buf[...], grads_buf[...]], axis=0)
    block = experts // SEND_CHUNKS
    count = block * capacity
    place = lax.broadcasted_iota(jnp.int32, (block, capacity, token_count), 1).astype(F32)
    sends = []
    for i in range(SEND_CHUNKS):
        start = i * block
        hit = keys[start : start + block, None, :] == place
        slots = jnp.where(hit, 1.0, 0.0).reshape(count, token_count).astype(BF16)
        slots_ref[i * count : (i + 1) * count, :] = slots
        weighted = jnp.where(hit, gates[start : start + block, None, :], 0.0)
        high, low = split_high_low(weighted.reshape(count, token_count))
        rows = dot(slots, tokens, 1, 0)
        scaled = dot(jnp.concatenate([high, low], axis=1), grads, 1, 0)
        here = slice(i * count, (i + 1) * count)
        send_buf[here, :width] = rows.astype(BF16)
        send_buf[here, width:] = scaled.astype(BF16)
        sends.append(
            pltpu.make_async_copy(send_buf.at[here], send_ref.at[here], send_sems.at[i])
        )
        sends[i].start()
        if i == 0:
            for copy in packing:
                copy.wait()
            packed_out = pltpu.make_async_copy(packed_buf, packed_ref, weight_sems.at[4])
            packed_out.start()
    for copy in [packed_out] + sends:
        copy.wait()


def expert_kernel(
    core_ref,
    recv_ref,
    weights_ref,
    parts_ref,
    grads_ref,
    gate_ref,
    ins_ref,
    rows_ref,
    down_ref,
    hidden_ref,
    stage_ref,
    row_sems,
    in_sems,
    out_sems,
):
    sources = gate_ref.shape[0]
    slot_count = rows_ref.shape[0]
    capacity = slot_count // sources
    pieces, _, depth, hidden_width = weights_ref.shape
    share = depth // 3
    half = share // 2
    width = pieces * share
    core = core_ref[0]

    def fetch(k, target):
        return pltpu.make_async_copy(
            weights_ref.at[:, core, k * share : (k + 1) * share, :], target, in_sems.at[k]
        )

    fetches = [
        fetch(0, ins_ref.at[:, :share, :]),
        fetch(1, ins_ref.at[:, share:, :]),
        fetch(2, down_ref),
    ]
    block = sources // CHUNKS
    count = block * capacity
    arrivals = [
        pltpu.make_async_copy(
            recv_ref.at[i * count : (i + 1) * count],
            rows_ref.at[i * count : (i + 1) * count],
            row_sems.at[i],
        )
        for i in range(CHUNKS)
    ]
    fetches[0].start()
    arrivals[0].start()
    fetches[1].start()
    fetches[2].start()
    fetches[0].wait()
    arrivals[0].wait()
    for copy in arrivals[1:]:
        copy.start()
    fetches[1].wait()
    fetches[2].wait()
    w_gate = ins_ref[:, :share, :].reshape(width, hidden_width)
    w_up = ins_ref[:, share:, :].reshape(width, hidden_width)
    down = jnp.concatenate(
        [
            down_ref[:, :half, :].reshape(hidden_width, hidden_width),
            down_ref[:, half:, :].reshape(hidden_width, hidden_width),
        ],
        axis=1,
    )
    tiles = capacity // TILE
    lane = lax.broadcasted_iota(jnp.int32, (block, TILE, PANEL), 2)

    def products(i):
        here = slice(i * count, (i + 1) * count)
        rows = rows_ref[here, :width]
        scaled = rows_ref[here, width:]
        return dot(rows, w_gate, 1, 0), dot(rows, w_up, 1, 0), dot(scaled, down, 1, 1)

    def activations(i, gate_pre, up_proj, hidden_grad):
        where = slice(i * count, (i + 1) * count)
        sig = jax.nn.sigmoid(gate_pre)
        act = gate_pre * sig
        hidden = (act * up_proj).astype(BF16)
        hidden_ref[where, :] = hidden
        grads_ref[where, hidden_width:] = (hidden_grad * act).astype(BF16)
        pre_grad = hidden_grad * up_proj * (sig + act * (1.0 - sig))
        grads_ref[where, :hidden_width] = pre_grad.astype(BF16)
        gate_grad = jnp.sum(hidden.astype(F32) * hidden_grad, axis=1, keepdims=True)
        gate_grad = gate_grad.reshape(block, tiles, TILE, 1)
        tile = jnp.zeros((block, TILE, PANEL), F32)
        for n in range(tiles):
            value = jnp.broadcast_to(gate_grad[:, n], (block, TILE, PANEL))
            high, low = split_high_low(value)
            tile = jnp.where(lane == 2 * n, high.astype(F32), tile)
            tile = jnp.where(lane == 2 * n + 1, low.astype(F32), tile)
        gate_ref[i * block : (i + 1) * block] = tile.astype(BF16)

    ahead = products(0)
    for i in range(CHUNKS):
        now = ahead
        if i + 1 < CHUNKS:
            arrivals[i + 1].wait()
            ahead = products(i + 1)
        activations(i, *now)

    def stores(k):
        return [
            pltpu.make_async_copy(
                stage_ref.at[k, c],
                parts_ref.at[:, core if c == 0 else 1 - core, k * share : (k + 1) * share, :],
                out_sems.at[k, c],
            )
            for c in range(2)
        ]

    sent = []
    rows = rows_ref[:, :width]
    for k in range(2):
        own = grads_ref[:, k * hidden_width : (k + 1) * hidden_width]
        total = dot(rows, own, 0, 0).astype(BF16)
        total = total.reshape(pieces // 2, 2, share, hidden_width)
        for c in range(2):
            stage_ref[k, c] = total[:, c]
        sent += stores(k)
        for copy in sent[-2:]:
            copy.start()
    scaled = rows_ref[:, width:]
    total = dot(hidden_ref[...], scaled, 0, 0).astype(BF16)
    for n in range(2):
        side = total[:, n * hidden_width : (n + 1) * hidden_width]
        side = side.reshape(pieces // 2, 2, half, hidden_width)
        for c in range(2):
            stage_ref[2, c, :, n * half : (n + 1) * half, :] = side[:, c]
    sent += stores(2)
    for copy in sent[-2:]:
        copy.start()
    for copy in sent:
        copy.wait()


def input_kernel(core_ref, grads_ref, gate_ref, weights_ref, back_ref, ins_ref, sem):
    sources, panels, _, _ = back_ref.shape
    share = weights_ref.shape[2] // 3
    pieces, _, hidden_width = ins_ref.shape
    core = core_ref[0]
    load = pltpu.make_async_copy(weights_ref.at[:, core, : 2 * share, :], ins_ref, sem)
    load.start()
    back_ref[:, panels - 1] = gate_ref[...]
    load.wait()
    width = pieces * share
    w_gate = ins_ref[:, :share, :].reshape(width, hidden_width)
    w_up = ins_ref[:, share:, :].reshape(width, hidden_width)
    weights = jnp.concatenate([w_gate, w_up], axis=1)
    block = sources // CHUNKS
    count = grads_ref.shape[0] // CHUNKS
    tiles = (panels - 1) * PANEL // width
    for i in range(CHUNKS):
        here = slice(i * block, (i + 1) * block)
        grad = dot(grads_ref[i * count : (i + 1) * count, :], weights, 1, 1).astype(BF16)
        for n in range(width // PANEL):
            panel = grad[:, n * PANEL : (n + 1) * PANEL]
            back_ref[here, n * tiles : (n + 1) * tiles] = panel.reshape(block, tiles, TILE, PANEL)


def combine_kernel(members, ids_ref, gates_ref, slots_ref, back_ref, input_ref, gate_ref):
    experts, panels, _, _ = back_ref.shape
    top, token_count = ids_ref.shape
    width = input_ref.shape[1]
    slot_count = slots_ref.shape[0]
    tiles = slot_count // (experts * TILE)
    slots = slots_ref[...]
    for n in range(width // PANEL):
        rows = back_ref[:, n * tiles : (n + 1) * tiles].reshape(slot_count, PANEL)
        input_ref[:, n * PANEL : (n + 1) * PANEL] = dot(slots, rows, 0, 0).astype(BF16)
    extra = back_ref[:, panels - 1].astype(F32)
    hits = slots.astype(F32).reshape(experts, tiles * TILE, token_count)
    by_expert = jnp.zeros((experts, token_count), F32)
    for n in range(tiles):
        value = extra[:, :, 2 * n : 2 * n + 1] + extra[:, :, 2 * n + 1 : 2 * n + 2]
        picked = jnp.where(hits[:, n * TILE : (n + 1) * TILE, :] > 0.0, value, 0.0)
        by_expert = by_expert + jnp.sum(picked, axis=1)
    expert = expert_of_row((experts, token_count), members)
    ids = ids_ref[...]
    for k in range(top):
        own = jnp.where(ids[k : k + 1, :] == expert, by_expert, 0.0)
        gate_ref[k : k + 1, :] = jnp.sum(own, axis=0, keepdims=True) / gates_ref[k : k + 1, :]


def scale_kernel(scale, core_ref, sums_ref, got_ref, gate_ref, up_ref, down_ref):
    share = gate_ref.shape[1]
    half = share // 2
    hidden_width = gate_ref.shape[2]
    core = core_ref[0]

    def put(member, value):
        value = (value.astype(F32) * scale)[None]
        here = pl.ds(member, 1)
        gate_ref[here] = value[:, :share]
        up_ref[here] = value[:, share : 2 * share]
        down_ref[here, :, :hidden_width] = value[:, 2 * share : 2 * share + half]
        down_ref[here, :, hidden_width:] = value[:, 2 * share + half :]

    put(core, sums_ref[0])
    put(1 - core, got_ref[1])


def shards(tokens, out_grad, route_ids, route_gates, w_gate, w_up, w_down):
    dp_size = lax.axis_size("dp")
    expert_size = lax.axis_size("expert")
    members, share, hidden_width = w_gate.shape
    experts = members * expert_size
    chips = dp_size // members
    depth = 3 * share
    token_count, top = route_ids.shape
    width = tokens.shape[1]
    capacity = 5 * token_count * top // (4 * experts)
    slot_count = experts * capacity
    scale = 1.0 / math.sqrt(token_count * dp_size * top / members)
    params = lambda mib: pltpu.CompilerParams(vmem_limit_bytes=mib * MIB)
    vmem = pl.BlockSpec(memory_space=pltpu.VMEM)
    smem = pl.BlockSpec(memory_space=pltpu.SMEM)
    anywhere = pl.BlockSpec(memory_space=pl.ANY)

    core = lax.rem(lax.axis_index("dp"), members).astype(jnp.int32).reshape(1)
    ids, core = lax.optimization_barrier((route_ids.T, core))
    gates = route_gates.T
    send, slots, packed = pl.pallas_call(
        functools.partial(dispatch_kernel, members, experts),
        in_specs=[vmem, vmem] + [anywhere] * 5,
        out_specs=(anywhere, vmem, anywhere),
        out_shape=(
            hbm_result(slot_count, 2 * width),
            vmem_result(slot_count, token_count),
            hbm_result(members, depth, hidden_width),
        ),
        scratch_shapes=[
            pltpu.VMEM((token_count, width), BF16),
            pltpu.VMEM((token_count, width), BF16),
            pltpu.VMEM((slot_count, 2 * width), BF16),
            pltpu.VMEM((members, depth, hidden_width), BF16),
            pltpu.SemaphoreType.DMA((5,)),
            pltpu.SemaphoreType.DMA((2,)),
            pltpu.SemaphoreType.DMA((SEND_CHUNKS,)),
        ],
        compiler_params=params(24),
        name="dispatch",
    )(in_hbm(ids), in_hbm(gates), *map(in_hbm, (tokens, out_grad, w_gate, w_up, w_down)))
    weights = lax.all_gather(packed, "dp", axis=0, tiled=False)

    chip_plane = [
        [(chip * members + c) * expert_size + e for c in range(members) for e in range(expert_size)]
        for chip in range(chips)
    ]

    def exchange(x):
        return lax.all_to_all(
            x,
            ("dp", "expert"),
            split_axis=0,
            concat_axis=0,
            tiled=True,
            axis_index_groups=chip_plane,
        )

    recv = exchange(send.reshape(experts, capacity, 2 * width)).reshape(slot_count, 2 * width)

    parts, row_grads, gate_tiles = pl.pallas_call(
        expert_kernel,
        in_specs=[smem, anywhere, anywhere],
        out_specs=(anywhere, vmem, vmem),
        out_shape=(
            hbm_result(chips, members, depth, hidden_width),
            vmem_result(slot_count, 2 * hidden_width),
            vmem_result(experts, TILE, PANEL),
        ),
        scratch_shapes=[
            pltpu.VMEM((dp_size, 2 * share, hidden_width), BF16),
            pltpu.VMEM((slot_count, 2 * width), BF16),
            pltpu.VMEM((dp_size, share, hidden_width), BF16),
            pltpu.VMEM((slot_count, hidden_width), BF16),
            pltpu.VMEM((3, members, chips, share, hidden_width), BF16),
            pltpu.SemaphoreType.DMA((CHUNKS,)),
            pltpu.SemaphoreType.DMA((3,)),
            pltpu.SemaphoreType.DMA((3, members)),
        ],
        compiler_params=params(40),
        name="expert",
    )(core, in_hbm(recv), in_hbm(weights))
    same_core = [list(range(c, dp_size, members)) for c in range(members)]
    sums = lax.psum_scatter(
        parts,
        "dp",
        scatter_dimension=0,
        tiled=False,
        axis_index_groups=same_core,
    )

    panels = capacity * width // (TILE * PANEL) + 1
    back = pl.pallas_call(
        input_kernel,
        in_specs=[smem, vmem, vmem, anywhere],
        out_specs=vmem,
        out_shape=vmem_result(experts, panels, TILE, PANEL),
        scratch_shapes=[
            pltpu.VMEM((dp_size, 2 * share, hidden_width), BF16),
            pltpu.SemaphoreType.DMA,
        ],
        compiler_params=params(24),
        name="inputs",
    )(core, in_vmem(row_grads), in_vmem(gate_tiles), in_hbm(weights))
    back, sums = lax.optimization_barrier((exchange(back), sums))
    got = lax.ppermute(sums, "dp", [(i, i ^ 1) for i in range(dp_size)])
    input_grad, gate_grad = pl.pallas_call(
        functools.partial(combine_kernel, members),
        out_shape=(
            jax.ShapeDtypeStruct((token_count, width), BF16),
            jax.ShapeDtypeStruct((top, token_count), F32),
        ),
        compiler_params=params(24),
        name="combine",
    )(ids, gates, in_vmem(slots), in_vmem(back))

    gate_sum, up_sum, down_sum = pl.pallas_call(
        functools.partial(scale_kernel, scale),
        in_specs=[smem, vmem, vmem],
        out_shape=tuple(jax.ShapeDtypeStruct(w.shape, F32) for w in (w_gate, w_up, w_down)),
        compiler_params=params(16),
        name="scale",
    )(core, sums, in_vmem(got))
    return (input_grad, gate_grad.T, gate_sum, up_sum, down_sum)


def solution(mesh):
    return jax.shard_map(
        shards,
        mesh=mesh,
        in_specs=(
            P(("dp", "expert"), None),
            P(("dp", "expert"), None),
            P(("dp", "expert"), None),
            P(("dp", "expert"), None),
            P("expert", "dp", None),
            P("expert", "dp", None),
            P("expert", "dp", None),
        ),
        out_specs=(
            P(("dp", "expert"), None),
            P(("dp", "expert"), None),
            P("expert", "dp", None),
            P("expert", "dp", None),
            P("expert", "dp", None),
        ),
        check_vma=False,
    )
```
